32 devices in a mesh: ens: 4 (over y, x), lat: 4 (over z), lon: 2 (over core).
Axes of the slice: x: 2, y: 2, z: 4, core: 2. Of those that a mesh axis runs over, the one named last changes fastest.
Arguments:
- hidden_state: bfloat16 [4, 90, 8, 720], P('ens', None, 'lat', 'lon'), may hold values from -6 to 6
- filter_coefficients: bfloat16 [9, 10, 90], replicated, may hold values from -0.21875 to 0.21875
- meridian_offset_table: int32 [3, 8], P(None, 'lat'), may hold values from 1 to 4
- function_pick_table: int32 [9, 8, 1440], P(None, 'lat', 'lon'), may hold values from 0 to 8
- observation: float32 [10, 8, 1440], P(None, 'lat', 'lon'), may hold values from -6 to 6
- latitude_cosine_factor: float32 [8], P('lat'), may hold values from 0.3 to 3
Outputs:
- latent_grad: float32 [4, 90, 8, 720], P('ens', None, 'lat', 'lon')
The draws below stay inside these ranges and needn't reach their ends.
All inputs are finite; a program needn't handle non-finite values.
Results may differ from the reference program's by a relative error of at most 0.0037.
Values may be sent and summed in bfloat16 or wider, within the bound.
No kernel may reach another device: no remote copies, remote signals or barrier semaphores. Data moves between devices by JAX's collectives and lax.ppermute only.
A program may use at most 64 MiB of HBM per device.

```python
import math
import jax
import jax.numpy as jnp
from jax import lax

C = 90
V = 10
NLON = 1440
BASES = 9
SPAN = 4
MEMBERS = 4
NLAT = 8
LLON = 720


def set_ends(values, stream_key, least, top_value):
    longest = values.shape.index(max(values.shape))
    spots = []
    for shift in (0, 1):
        where = [jax.random.randint(jax.random.fold_in(stream_key, axis), (), 0, length) for axis, length in enumerate(values.shape)]
        where[longest] = (where[longest] + shift) % values.shape[longest]
        spots.append(tuple(where))
    return values.at[spots[0]].set(least).at[spots[1]].set(top_value)


def block_scale(own_key, shape, pieces, low, top_value):
    factor_of, own = 1.0, jax.random.fold_in(own_key, 6)
    for axis_at, blocks in pieces:
        steps = jnp.exp(jax.random.uniform(jax.random.fold_in(own, axis_at), (blocks,), jnp.float32, low / len(pieces), top_value / len(pieces)))
        factor_of = factor_of * jnp.repeat(steps, shape[axis_at] // blocks).reshape([-1 if axis == axis_at else 1 for axis in range(len(shape))])
    return factor_of


def gaussian(stream_key, dims, width, limit, split=(), held_as=jnp.bfloat16):
    drawn = width * jax.random.normal(stream_key, dims, jnp.float32)
    if split:
        drawn = drawn * block_scale(stream_key, dims, split, -0.22, 0.18)
    return jnp.clip(drawn, -limit, limit).astype(held_as)


def setup_inputs(seed: int = 0) -> dict:
    seeds = jax.random.split(jax.random.key(seed), 7)
    hidden_state = gaussian(seeds[0], (MEMBERS, C, NLAT, LLON), 1.0, 6.0, ((0, 4), (2, 4), (3, 2)))
    filter_coefficients = gaussian(seeds[1], (BASES, V, C), (BASES * C) ** -0.5, 0.21875)
    meridian_offset_table = set_ends(jax.random.randint(seeds[2], (3, NLAT), 1, SPAN + 1), jax.random.fold_in(seeds[2], 1), 1, SPAN).astype(jnp.int32)
    function_pick_table = set_ends(jax.random.randint(seeds[3], (BASES, NLAT, NLON), 0, BASES), jax.random.fold_in(seeds[3], 1), 0, BASES - 1).astype(jnp.int32)
    observation = gaussian(seeds[4], (V, NLAT, NLON), 1.0, 6.0, ((1, 4), (2, 2)), jnp.float32)
    latitude_cosine_factor = jnp.clip(jnp.exp(math.log(3.0) - 2.3025851 * jax.random.uniform(seeds[5], (NLAT,), jnp.float32) ** block_scale(seeds[5], (NLAT,), ((0, 4),), -0.2, 0.2)), 0.3, 3.0)
    return {"hidden_state": hidden_state, "filter_coefficients": filter_coefficients, "meridian_offset_table": meridian_offset_table, "function_pick_table": function_pick_table, "observation": observation, "latitude_cosine_factor": latitude_cosine_factor}


smooth_square = 0.01

def smoothed_derivative(difference):
    return difference / jnp.sqrt(difference * difference + smooth_square)

def shift_rows(values, offset):
    parallel_number = values.shape[-2]
    widths = [(0, 0)] * (values.ndim - 2)
    if offset > 0:
        padded = jnp.pad(values, widths + [(0, offset), (0, 0)])
        return padded[..., offset:offset + parallel_number, :]
    if offset < 0:
        padded = jnp.pad(values, widths + [(-offset, 0), (0, 0)])
        return padded[..., :parallel_number, :]
    return values

def predict(member_latent, filter_coefficients, meridian_offset_table, function_pick_table):
    basis_count, variables, channels = filter_coefficients.shape
    parallel_number = member_latent.shape[1]
    meridian_number = member_latent.shape[2] * 2
    latent_f32 = member_latent.astype(jnp.float32)
    halfway = 0.5 * (latent_f32 + jnp.roll(latent_f32, -1, axis=-1))
    interpolated = jnp.stack([latent_f32, halfway], axis=-1).reshape(channels, parallel_number, meridian_number).astype(jnp.bfloat16)
    product = jnp.dot(filter_coefficients.reshape(basis_count * variables, channels), interpolated.reshape(channels, -1), preferred_element_type=jnp.float32)
    product = product.reshape(basis_count, variables, parallel_number, meridian_number)
    columns = jnp.arange(meridian_number, dtype=jnp.int32)
    levels = jnp.arange(basis_count, dtype=jnp.int32)
    result = jnp.zeros((variables, parallel_number, meridian_number), jnp.float32)
    for row_step in (-1, 0, 1):
        shifted = shift_rows(product, row_step)
        for col_step in (-1, 0, 1):
            adjacent_position = 3 * (row_step + 1) + col_step + 1
            target_cols = (columns[None, :] + col_step * meridian_offset_table[row_step + 1][:, None]) % meridian_number
            picked = jnp.take_along_axis(shifted, jnp.broadcast_to(target_cols[None, None], shifted.shape), axis=3)
            picked_function = (function_pick_table[adjacent_position][None] == levels[:, None, None]).astype(jnp.float32)
            result = result + lax.optimization_barrier(jnp.sum(picked_function[:, None] * picked, axis=0))
    return result

def hidden_derivative_accum(prediction_derivative, filter_coefficients, meridian_offset_table, function_pick_table):
    basis_count, variables, channels = filter_coefficients.shape
    parallel_number = prediction_derivative.shape[1]
    meridian_number = prediction_derivative.shape[2]
    columns = jnp.arange(meridian_number, dtype=jnp.int32)
    levels = jnp.arange(basis_count, dtype=jnp.int32)
    product_grad = jnp.zeros((basis_count, variables, parallel_number, meridian_number), jnp.float32)
    for row_step in (-1, 0, 1):
        collected = jnp.zeros((basis_count, variables, parallel_number, meridian_number), jnp.float32)
        for col_step in (-1, 0, 1):
            adjacent_position = 3 * (row_step + 1) + col_step + 1
            picked_function = (function_pick_table[adjacent_position][None] == levels[:, None, None]).astype(jnp.float32)
            sample_dispersion = picked_function[:, None] * prediction_derivative[None]
            source_cols = (columns[None, :] - col_step * meridian_offset_table[row_step + 1][:, None]) % meridian_number
            collected = collected + jnp.take_along_axis(sample_dispersion, jnp.broadcast_to(source_cols[None, None], sample_dispersion.shape), axis=3)
        product_grad = product_grad + shift_rows(collected, -row_step)
    flat_weight = filter_coefficients.reshape(basis_count * variables, channels).astype(jnp.float32)
    field_grad = jnp.dot(flat_weight.T, product_grad.reshape(basis_count * variables, -1), precision=lax.Precision.HIGHEST)
    paired = field_grad.reshape(channels, parallel_number, meridian_number // 2, 2)
    even_part = paired[..., 0]
    odd_part = paired[..., 1]
    return even_part + 0.5 * odd_part + 0.5 * jnp.roll(odd_part, 1, axis=-1)

def reference(hidden_state, filter_coefficients, meridian_offset_table, function_pick_table, observation, latitude_cosine_factor):

    def decode_sample(member_latent):
        return predict(member_latent, filter_coefficients, meridian_offset_table, function_pick_table)
    prediction_fields = lax.map(decode_sample, hidden_state)
    sample_number = prediction_fields.shape[0]

    def couple_accumulated(sample_outputs):
        return lax.optimization_barrier(jnp.sum(smoothed_derivative(sample_outputs[None] - prediction_fields), axis=0))
    sample_couples = lax.map(couple_accumulated, prediction_fields)
    prediction_derivative = latitude_cosine_factor[None, None, :, None] * (smoothed_derivative(prediction_fields - observation[None]) - sample_couples / (sample_number - 1))

    def sample_reverse_sweep(member_grad):
        return hidden_derivative_accum(member_grad, filter_coefficients, meridian_offset_table, function_pick_table)
    return lax.map(sample_reverse_sweep, prediction_derivative)
```

```python
import functools

import jax
import jax.numpy as jnp
from jax import lax
from jax.experimental import pallas as pl
from jax.experimental.pallas import tpu as pltpu
from jax.sharding import PartitionSpec as P

SPAN = 4
MARGIN = SPAN + 1
LANES = 128
SUB = 16

smooth_square = 0.01

f32 = jnp.float32
bf16 = jnp.bfloat16
VMEM = pl.BlockSpec(memory_space=pltpu.VMEM)


def up_to(n, step):
    return -(-n // step) * step


class Sizes:
    def __init__(self, hidden, filt):
        _, self.channels, self.rows, self.cols = hidden.shape
        self.bases, self.variables, _ = filt.shape
        self.slots = 9
        self.lanes = up_to(self.cols + 2 * MARGIN, LANES)
        self.rim = (self.cols - MARGIN) // LANES * LANES
        self.latent_rows = up_to(self.channels * self.rows, SUB)
        self.pick_rows = up_to(self.slots + 5, SUB)
        self.obs_rows = up_to(self.variables, SUB)
        self.half = self.pick_rows + 2 * self.obs_rows
        self.table = 2 * self.half
        self.own_rows = self.latent_rows + self.rows * self.table
        self.message = self.latent_rows + self.table
        self.dest = self.rows + 2
        self.source = self.rows + 4
        self.vpad = up_to(self.variables, 8)
        self.wrows = self.bases * self.vpad
        self.blocks = 2 * self.dest
        self.full = self.variables // 8 * 8
        self.rest = self.variables - self.full
        self.packed = self.blocks * self.full + up_to(self.blocks * self.rest, 8)


def lane_roll(x, shift, lanes):
    if isinstance(shift, int):
        return x if shift % lanes == 0 else pltpu.roll(x, shift % lanes, axis=1)
    return pltpu.roll(x, jnp.where(shift < 0, shift + lanes, shift), axis=1)


def prepare_kernel(z, hidden, pick, obs, offsets, cosine, own, edge, work):
    h = hidden[0].reshape(z.channels * z.rows, z.cols)
    own[0 : z.latent_rows] = jnp.pad(
        h, ((0, z.latent_rows - z.channels * z.rows), (0, z.lanes - z.cols))
    )
    wide = 2 * LANES
    row = lax.broadcasted_iota(jnp.int32, (wide, wide), 0)
    col = lax.broadcasted_iota(jnp.int32, (wide, wide), 1)
    split = (row == jnp.where(col < LANES, 2 * col, 2 * (col - LANES) + 1)).astype(f32).astype(bf16)
    work[...] = jnp.zeros_like(work)
    grid = 2 * z.cols
    for i in range(z.rows):
        work[0 : z.slots, 0:grid] = pick[:, i, :].astype(f32)
        o = obs[:, i, :]
        high = o.astype(bf16).astype(f32)
        work[z.pick_rows : z.pick_rows + z.variables, 0:grid] = high
        low_at = z.pick_rows + z.obs_rows
        work[low_at : low_at + z.variables, 0:grid] = o - high
        for t in range(3):
            work[z.slots + t : z.slots + t + 1, :] = jnp.broadcast_to(
                offsets[i : i + 1, t : t + 1].astype(f32), (1, work.shape[1])
            )
        c = cosine[0:1, i : i + 1]
        c_high = c.astype(bf16).astype(f32)
        work[z.slots + 3 : z.slots + 4, :] = jnp.broadcast_to(c_high, (1, work.shape[1]))
        work[z.slots + 4 : z.slots + 5, :] = jnp.broadcast_to(c - c_high, (1, work.shape[1]))
        at = z.latent_rows + i * z.table
        for n in range(z.lanes // LANES):
            parts = jnp.dot(
                work[:, n * wide : (n + 1) * wide].astype(bf16), split, preferred_element_type=f32
            ).astype(bf16)
            for parity in range(2):
                own[at + parity * z.half : at + (parity + 1) * z.half, n * LANES : (n + 1) * LANES] = (
                    parts[:, parity * LANES : (parity + 1) * LANES]
                )
    width = z.lanes - z.rim
    lane = lax.broadcasted_iota(jnp.int32, (z.own_rows, width), 1)
    first = pltpu.roll(own[:, 0:width].astype(f32), z.cols - z.rim, axis=1)
    last = pltpu.roll(own[:, z.rim :].astype(f32), z.lanes - z.cols, axis=1)
    ahead = (lane >= z.cols - z.rim) & (lane < z.cols - z.rim + MARGIN)
    behind = lane >= width - MARGIN
    edge[...] = jnp.where(ahead, first, jnp.where(behind, last, 0.0)).astype(bf16)


def merge_kernel(z, own, right, left, whole, one, two):
    whole[:, 0 : z.rim] = own[:, 0 : z.rim]
    width = z.lanes - z.rim
    lane = lax.broadcasted_iota(jnp.int32, (z.own_rows, width), 1)
    behind = lane >= width - MARGIN
    outer = jnp.where(behind, left[...].astype(f32), right[...].astype(f32))
    inner = own[:, z.rim :].astype(f32)
    whole[:, z.rim :] = jnp.where(lane < z.cols - z.rim, inner, outer).astype(bf16)
    odd = lax.rem(lax.axis_index("lat"), 2)
    last = z.rows - 1
    for message, row in ((one, last - last * odd), (two, last * odd)):
        message[0 : z.latent_rows] = whole[0 : z.latent_rows]
        at = pl.multiple_of(z.latent_rows + row * z.table, SUB)
        message[z.latent_rows :] = whole[pl.ds(at, z.table)]


def scalar_of(row):
    return jnp.max(row).astype(jnp.int32)


def steps(direction, offset, parity):
    if direction == 0:
        return parity, 0
    distance = direction * offset
    other = lax.rem(parity + offset, 2)
    return other, lax.shift_right_arithmetic(distance + other - parity, 1)


def forward_kernel(z, own, one, two, filt, packed, picks, weight, step_table, near, table, product, chosen, wide_w):
    odd = lax.rem(lax.axis_index("lat"), 2)

    for part in range(0, z.message, SUB):
        a = one[part : part + SUB].astype(f32)
        b = two[part : part + SUB].astype(f32)
        near[0, part : part + SUB] = jnp.where(odd == 1, a, b).astype(bf16)
        near[1, part : part + SUB] = jnp.where(odd == 1, b, a).astype(bf16)

    def table_rows(i, parity, start, count):
        at = parity * z.half + start
        if i == 0:
            return near[0, z.latent_rows + at : z.latent_rows + at + count].astype(f32)
        if i == z.dest - 1:
            return near[1, z.latent_rows + at : z.latent_rows + at + count].astype(f32)
        at += z.latent_rows + (i - 1) * z.table
        return own[at : at + count].astype(f32)

    for i in range(z.dest):
        for parity in range(2):
            table[2 * i + parity] = table_rows(i, parity, 0, z.pick_rows)
    offset = [
        [scalar_of(table[2 * i, z.slots + t : z.slots + t + 1, 0:LANES]) for t in range(3)]
        for i in range(z.dest)
    ]
    for i in range(z.dest):
        for t in range(3):
            step_table[3 * i + t] = offset[i][t]

    wide_w[...] = jnp.zeros_like(wide_w)
    for k in range(z.bases):
        wide_w[k * z.vpad : k * z.vpad + z.variables, 0 : z.channels] = filt[k].astype(f32)
    flat = wide_w[...].astype(bf16)
    c_at = lax.broadcasted_iota(jnp.int32, (LANES, z.latent_rows), 0)
    r_at = lax.broadcasted_iota(jnp.int32, (LANES, z.latent_rows), 1)
    for i in range(z.rows):
        spread = (r_at == c_at * z.rows + i).astype(f32).astype(bf16)
        weight[i * z.wrows : (i + 1) * z.wrows] = jnp.dot(
            flat, spread, preferred_element_type=f32
        ).astype(bf16)

    def multiply(latents, rows_at):
        h = latents.astype(f32)
        halfway = (0.5 * (h + pltpu.roll(h, z.lanes - 1, axis=1))).astype(bf16)
        for i, r in rows_at:
            w = weight[i * z.wrows : (i + 1) * z.wrows]
            product[2 * r] = jnp.dot(w, latents, preferred_element_type=f32)
            product[2 * r + 1] = jnp.dot(w, halfway, preferred_element_type=f32)

    multiply(own[0 : z.latent_rows], [(i, i + 2) for i in range(z.rows)])
    multiply(near[0, 0 : z.latent_rows], [(z.rows - 2 + n, n) for n in range(2)])
    multiply(near[1, 0 : z.latent_rows], [(n, z.rows + 2 + n) for n in range(2)])

    def instance(i, a, b):
        return (i * 9 + 3 * (a + 1) + b + 1) * 2

    for r in range(z.source):
        for parity in range(2):
            work = []
            for a in (-1, 0, 1):
                i = r - 1 - a
                if not 0 <= i < z.dest:
                    continue
                for b in (-1, 0, 1):
                    slot = 3 * (a + 1) + b + 1
                    n = instance(i, a, b) + parity
                    other, shift = steps(b, offset[i][a + 1], parity)
                    row = table[2 * i + other, slot : slot + 1, :]
                    picks[n : n + 1, :] = lane_roll(row, shift, z.lanes)
                    work.append(n)
            for lane in range(0, z.lanes, LANES):
                at = slice(lane, lane + LANES)
                pick = [jnp.broadcast_to(picks[n : n + 1, at], (8, LANES)) for n in work]
                for k in range(z.bases):
                    mask = [p == float(k) for p in pick] if k else None
                    for v in range(0, z.vpad, 8):
                        value = product[2 * r + parity, k * z.vpad + v : k * z.vpad + v + 8, at]
                        if k == 0:
                            if v == 0:
                                best = {}
                            for m in range(len(work)):
                                best[m, v] = value
                        else:
                            for m in range(len(work)):
                                best[m, v] = jnp.where(mask[m], value, best[m, v])
                for m, n in enumerate(work):
                    for v in range(0, z.vpad, 8):
                        chosen[n, v : v + 8, at] = best[m, v]

    packed[...] = jnp.zeros_like(packed)
    for i in range(z.dest):
        for parity in range(2):
            total = None
            for a in (-1, 0, 1):
                for b in (-1, 0, 1):
                    other, shift = steps(-b, offset[i][a + 1], parity)
                    value = lane_roll(chosen[instance(i, a, b) + other], shift, z.lanes)
                    total = value if total is None else total + value
            block = 2 * i + parity
            if z.full:
                packed[block * z.full : (block + 1) * z.full] = total[0 : z.full]
            if z.rest:
                at = z.blocks * z.full + block * z.rest
                packed[at : at + z.rest] = total[z.full : z.variables]


def smoothed_derivative(difference):
    return difference * lax.rsqrt(difference * difference + smooth_square)


def backward_kernel(z, members, *refs):
    mine, others = refs[0], refs[1:members]
    own, one, two, picks, weight, step_table, out, obs, scale, grad, hi, lo, hi_odd, lo_odd = refs[members:]
    odd = lax.rem(lax.axis_index("lat"), 2)

    def table_rows(i, parity, start, count):
        at = parity * z.half + start
        if i == 0 or i == z.dest - 1:
            at += z.latent_rows
            a = one[at : at + count].astype(f32)
            b = two[at : at + count].astype(f32)
            return jnp.where(odd == 1, a, b) if i == 0 else jnp.where(odd == 1, b, a)
        at += z.latent_rows + (i - 1) * z.table
        return own[at : at + count].astype(f32)

    obs[...] = jnp.zeros_like(obs)
    scale[...] = jnp.zeros_like(scale)
    for i in range(z.dest):
        head = table_rows(i, 0, 0, z.pick_rows)
        cosine = head[z.slots + 3 : z.slots + 4] + head[z.slots + 4 : z.slots + 5]
        for parity in range(2):
            high = table_rows(i, parity, z.pick_rows, z.obs_rows)
            low = table_rows(i, parity, z.pick_rows + z.obs_rows, z.obs_rows)
            value = high + low
            block = 2 * i + parity
            if z.full:
                obs[block * z.full : (block + 1) * z.full] = value[0 : z.full]
                scale[block * z.full : (block + 1) * z.full] = jnp.broadcast_to(cosine, (z.full, z.lanes))
            if z.rest:
                at = z.blocks * z.full + block * z.rest
                obs[at : at + z.rest] = value[z.full : z.variables]
                scale[at : at + z.rest] = jnp.broadcast_to(cosine, (z.rest, z.lanes))
    value = mine[...]
    pairs = None
    for other in others:
        term = smoothed_derivative(value - other[...])
        pairs = term if pairs is None else pairs + term
    result = smoothed_derivative(value - obs[...])
    if pairs is not None:
        result = result - pairs * (1.0 / (members - 1))
    obs[...] = scale[...] * result
    grad[...] = jnp.zeros_like(grad)
    for block in range(z.blocks):
        if z.full:
            grad[block, 0 : z.full] = obs[block * z.full : (block + 1) * z.full]
        if z.rest:
            at = z.blocks * z.full + block * z.rest
            grad[block, z.full : z.variables] = obs[at : at + z.rest]

    for j in range(1, z.rows + 1):
        moved = {}
        for parity in range(2):
            for a in (-1, 0, 1):
                i = j - a
                for b in (-1, 0, 1):
                    other, shift = steps(b, step_table[3 * i + a + 1], parity)
                    moved[parity, a, b] = lane_roll(grad[2 * i + other], shift, z.lanes)
        for lane in range(0, z.lanes, LANES):
            at = slice(lane, lane + LANES)
            pick = {}
            for (parity, a, b) in moved:
                n = ((j - a) * 9 + 3 * (a + 1) + b + 1) * 2 + parity
                pick[parity, a, b] = jnp.broadcast_to(picks[n : n + 1, at], (8, LANES))
            for k in range(z.bases):
                total = {}
                for key, p in pick.items():
                    mask = p == float(k)
                    for v in range(0, z.vpad, 8):
                        term = jnp.where(mask, moved[key][v : v + 8, at], 0.0)
                        old = total.get((key[0], v))
                        total[key[0], v] = term if old is None else old + term
                for v in range(0, z.vpad, 16):
                    even = jnp.concatenate([total[0, v], total[0, v + 8]], axis=0)
                    half = 0.5 * jnp.concatenate([total[1, v], total[1, v + 8]], axis=0)
                    even = even + half
                    rows = slice((j - 1) * z.wrows + k * z.vpad + v, (j - 1) * z.wrows + k * z.vpad + v + 16)
                    top = even.astype(bf16)
                    hi[rows, at] = top
                    lo[rows, at] = (even - top.astype(f32)).astype(bf16)
                    top = half.astype(bf16)
                    hi_odd[rows, at] = top
                    lo_odd[rows, at] = (half - top.astype(f32)).astype(bf16)
    w = weight[...]
    contract = (((0,), (0,)), ((), ()))

    def multiply(x):
        return lax.dot_general(w, x, contract, preferred_element_type=f32)

    here = multiply(hi[...]) + multiply(lo[...])
    behind = multiply(hi_odd[...]) + multiply(lo_odd[...])
    field = here + pltpu.roll(behind, 1, axis=1)
    out[0] = field[0 : z.channels * z.rows, 0 : z.cols].reshape(z.channels, z.rows, z.cols)


def swaps(count, start):
    pairs = []
    for i in range(start, count - 1, 2):
        pairs += [(i, i + 1), (i + 1, i)]
    return pairs


def call(name, kernel, outs, scratch=(), out_specs=None, in_specs=None, inputs=()):
    size = sum(x.size * x.dtype.itemsize for x in tuple(inputs) + tuple(outs))
    return pl.pallas_call(
        kernel,
        name=name,
        out_shape=tuple(outs),
        in_specs=in_specs or [VMEM] * len(inputs),
        out_specs=out_specs or tuple([VMEM] * len(outs)),
        scratch_shapes=list(scratch),
        cost_estimate=pl.CostEstimate(flops=100_000_000, bytes_accessed=size, transcendentals=0),
    )(*inputs)


def on_device(hidden, filt, offsets, pick, observation, cosine):
    z = Sizes(hidden, filt)
    shape = jax.ShapeDtypeStruct
    own, edge = call(
        "prepare",
        functools.partial(prepare_kernel, z),
        [shape((z.own_rows, z.lanes), bf16), shape((z.own_rows, z.lanes - z.rim), bf16)],
        [pltpu.VMEM((z.half, 2 * z.lanes), f32)],
        inputs=(hidden, pick, observation, offsets.T, cosine[None]),
    )
    count = lax.axis_size("lon")
    right = lax.ppermute(edge, "lon", [((i + 1) % count, i) for i in range(count)])
    left = right
    if count != 2:
        left = lax.ppermute(edge, "lon", [(i, (i + 1) % count) for i in range(count)])
    whole, first, second = call(
        "merge",
        functools.partial(merge_kernel, z),
        [shape((z.own_rows, z.lanes), bf16)] + [shape((z.message, z.lanes), bf16)] * 2,
        inputs=(own, right, left),
    )
    count = lax.axis_size("lat")
    one = lax.ppermute(first, "lat", swaps(count, 0))
    two = lax.ppermute(second, "lat", swaps(count, 1))
    instances = z.dest * 9 * 2
    smem = pl.BlockSpec(memory_space=pltpu.SMEM)
    packed, picks, weight, step_table = call(
        "forward",
        functools.partial(forward_kernel, z),
        [
            shape((z.packed, z.lanes), f32),
            shape((instances, z.lanes), f32),
            shape((z.rows * z.wrows, z.latent_rows), bf16),
            shape((3 * z.dest,), jnp.int32),
        ],
        [
            pltpu.VMEM((2, z.message, z.lanes), bf16),
            pltpu.VMEM((z.blocks, z.pick_rows, z.lanes), f32),
            pltpu.VMEM((2 * z.source, z.wrows, z.lanes), f32),
            pltpu.VMEM((instances, z.vpad, z.lanes), f32),
            pltpu.VMEM((z.wrows, LANES), f32),
        ],
        out_specs=(VMEM, VMEM, VMEM, smem),
        inputs=(whole, one, two, filt),
    )
    members = lax.axis_size("ens")
    others = []
    for k in range(1, members):
        if members & (members - 1):
            route = [(i, (i + k) % members) for i in range(members)]
        else:
            route = [(i, i ^ k) for i in range(members)]
        others.append(lax.ppermute(packed, "ens", route))
    inputs = (packed, *others, whole, one, two, picks, weight, step_table)
    (result,) = call(
        "backward",
        functools.partial(backward_kernel, z, members),
        [shape(hidden.shape, f32)],
        [
            pltpu.VMEM((z.packed, z.lanes), f32),
            pltpu.VMEM((z.packed, z.lanes), f32),
            pltpu.VMEM((z.blocks, z.vpad, z.lanes), f32),
        ]
        + [pltpu.VMEM((z.rows * z.wrows, z.lanes), bf16)] * 4,
        in_specs=[VMEM] * (len(inputs) - 1) + [smem],
        inputs=inputs,
    )
    return result


def solution(mesh):
    return jax.shard_map(
        on_device,
        mesh=mesh,
        in_specs=(
            P("ens", None, "lat", "lon"),
            P(),
            P(None, "lat"),
            P(None, "lat", "lon"),
            P(None, "lat", "lon"),
            P("lat"),
        ),
        out_specs=P("ens", None, "lat", "lon"),
        check_vma=False,
    )
```

```python
import functools

import jax
import jax.numpy as jnp
from jax import lax
from jax.experimental import pallas as pl
from jax.experimental.pallas import tpu as pltpu
from jax.sharding import PartitionSpec as P

SPAN = 4
MARGIN = SPAN + 1
LANES = 128
SUB = 16
VMEM_LIMIT = 16 * 2**20

smooth_square = 0.01

f32 = jnp.float32
bf16 = jnp.bfloat16
VMEM = pl.BlockSpec(memory_space=pltpu.VMEM)


def up_to(n, step):
    return -(-n // step) * step


class Sizes:
    def __init__(self, hidden, filt):
        _, self.channels, self.rows, self.cols = hidden.shape
        self.bases, self.variables, _ = filt.shape
        self.slots = 9
        self.lanes = up_to(self.cols + 2 * MARGIN, LANES)
        self.rim = (self.cols - MARGIN) // LANES * LANES
        self.latent_rows = up_to(self.channels * self.rows, SUB)
        self.pick_rows = up_to(self.slots + 5, SUB)
        self.obs_rows = up_to(self.variables, SUB)
        self.half = self.pick_rows + 2 * self.obs_rows
        self.table = 2 * self.half
        self.own_rows = self.latent_rows + self.rows * self.table
        self.message = self.latent_rows + self.table
        self.dest = self.rows + 2
        self.source = self.rows + 4
        self.vpad = up_to(self.variables, 8)
        self.wrows = self.bases * self.vpad
        self.blocks = 2 * self.dest
        self.full = self.variables // 8 * 8
        self.rest = self.variables - self.full
        self.packed = self.blocks * self.full + up_to(self.blocks * self.rest, 8)


def lane_roll(x, shift, lanes):
    if isinstance(shift, int):
        return x if shift % lanes == 0 else pltpu.roll(x, shift % lanes, axis=1)
    return pltpu.roll(x, jnp.where(shift < 0, shift + lanes, shift), axis=1)


def prepare_kernel(z, hidden, pick, obs, offsets, cosine, own, edge, work):
    h = hidden[0].reshape(z.channels * z.rows, z.cols)
    own[0 : z.latent_rows] = jnp.pad(
        h, ((0, z.latent_rows - z.channels * z.rows), (0, z.lanes - z.cols))
    )
    wide = 2 * LANES
    row = lax.broadcasted_iota(jnp.int32, (wide, wide), 0)
    col = lax.broadcasted_iota(jnp.int32, (wide, wide), 1)
    split = (row == jnp.where(col < LANES, 2 * col, 2 * (col - LANES) + 1)).astype(f32).astype(bf16)
    work[...] = jnp.zeros_like(work)
    grid = 2 * z.cols
    for i in range(z.rows):
        work[0 : z.slots, 0:grid] = pick[:, i, :].astype(f32)
        o = obs[:, i, :]
        high = o.astype(bf16).astype(f32)
        work[z.pick_rows : z.pick_rows + z.variables, 0:grid] = high
        low_at = z.pick_rows + z.obs_rows
        work[low_at : low_at + z.variables, 0:grid] = o - high
        for t in range(3):
            work[z.slots + t : z.slots + t + 1, :] = jnp.broadcast_to(
                offsets[i : i + 1, t : t + 1].astype(f32), (1, work.shape[1])
            )
        c = cosine[0:1, i : i + 1]
        c_high = c.astype(bf16).astype(f32)
        work[z.slots + 3 : z.slots + 4, :] = jnp.broadcast_to(c_high, (1, work.shape[1]))
        work[z.slots + 4 : z.slots + 5, :] = jnp.broadcast_to(c - c_high, (1, work.shape[1]))
        at = z.latent_rows + i * z.table
        for n in range(z.lanes // LANES):
            parts = jnp.dot(
                work[:, n * wide : (n + 1) * wide].astype(bf16), split, preferred_element_type=f32
            ).astype(bf16)
            for parity in range(2):
                own[at + parity * z.half : at + (parity + 1) * z.half, n * LANES : (n + 1) * LANES] = (
                    parts[:, parity * LANES : (parity + 1) * LANES]
                )
    width = z.lanes - z.rim
    lane = lax.broadcasted_iota(jnp.int32, (z.own_rows, width), 1)
    first = pltpu.roll(own[:, 0:width].astype(f32), z.cols - z.rim, axis=1)
    last = pltpu.roll(own[:, z.rim :].astype(f32), z.lanes - z.cols, axis=1)
    ahead = (lane >= z.cols - z.rim) & (lane < z.cols - z.rim + MARGIN)
    behind = lane >= width - MARGIN
    edge[...] = jnp.where(ahead, first, jnp.where(behind, last, 0.0)).astype(bf16)


def merge_kernel(z, own, right, left, whole, one, two):
    whole[:, 0 : z.rim] = own[:, 0 : z.rim]
    width = z.lanes - z.rim
    lane = lax.broadcasted_iota(jnp.int32, (z.own_rows, width), 1)
    behind = lane >= width - MARGIN
    outer = jnp.where(behind, left[...].astype(f32), right[...].astype(f32))
    inner = own[:, z.rim :].astype(f32)
    whole[:, z.rim :] = jnp.where(lane < z.cols - z.rim, inner, outer).astype(bf16)
    odd = lax.rem(lax.axis_index("lat"), 2)
    last = z.rows - 1
    for message, row in ((one, last - last * odd), (two, last * odd)):
        message[0 : z.latent_rows] = whole[0 : z.latent_rows]
        at = pl.multiple_of(z.latent_rows + row * z.table, SUB)
        message[z.latent_rows :] = whole[pl.ds(at, z.table)]


def scalar_of(row):
    return jnp.max(row).astype(jnp.int32)


def steps(direction, offset, parity):
    if direction == 0:
        return parity, 0
    distance = direction * offset
    other = lax.rem(parity + offset, 2)
    return other, lax.shift_right_arithmetic(distance + other - parity, 1)


def forward_kernel(z, own, one, two, filt, packed, picks, weight, step_table, near, table, product, chosen, wide_w):
    odd = lax.rem(lax.axis_index("lat"), 2)

    for part in range(0, z.message, SUB):
        a = one[part : part + SUB].astype(f32)
        b = two[part : part + SUB].astype(f32)
        near[0, part : part + SUB] = jnp.where(odd == 1, a, b).astype(bf16)
        near[1, part : part + SUB] = jnp.where(odd == 1, b, a).astype(bf16)

    def table_rows(i, parity, start, count):
        at = parity * z.half + start
        if i == 0:
            return near[0, z.latent_rows + at : z.latent_rows + at + count].astype(f32)
        if i == z.dest - 1:
            return near[1, z.latent_rows + at : z.latent_rows + at + count].astype(f32)
        at += z.latent_rows + (i - 1) * z.table
        return own[at : at + count].astype(f32)

    for i in range(z.dest):
        for parity in range(2):
            table[2 * i + parity] = table_rows(i, parity, 0, z.pick_rows)
    offset = [
        [scalar_of(table[2 * i, z.slots + t : z.slots + t + 1, 0:LANES]) for t in range(3)]
        for i in range(z.dest)
    ]
    for i in range(z.dest):
        for t in range(3):
            step_table[3 * i + t] = offset[i][t]

    wide_w[...] = jnp.zeros_like(wide_w)
    for k in range(z.bases):
        wide_w[k * z.vpad : k * z.vpad + z.variables, 0 : z.channels] = filt[k].astype(f32)
    flat = wide_w[...].astype(bf16)
    c_at = lax.broadcasted_iota(jnp.int32, (LANES, z.latent_rows), 0)
    r_at = lax.broadcasted_iota(jnp.int32, (LANES, z.latent_rows), 1)
    for i in range(z.rows):
        spread = (r_at == c_at * z.rows + i).astype(f32).astype(bf16)
        weight[i * z.wrows : (i + 1) * z.wrows] = jnp.dot(
            flat, spread, preferred_element_type=f32
        ).astype(bf16)

    def multiply(latents, rows_at):
        h = latents.astype(f32)
        halfway = (0.5 * (h + pltpu.roll(h, z.lanes - 1, axis=1))).astype(bf16)
        for i, r in rows_at:
            w = weight[i * z.wrows : (i + 1) * z.wrows]
            product[2 * r] = jnp.dot(w, latents, preferred_element_type=f32)
            product[2 * r + 1] = jnp.dot(w, halfway, preferred_element_type=f32)

    multiply(own[0 : z.latent_rows], [(i, i + 2) for i in range(z.rows)])
    multiply(near[0, 0 : z.latent_rows], [(z.rows - 2 + n, n) for n in range(2)])
    multiply(near[1, 0 : z.latent_rows], [(n, z.rows + 2 + n) for n in range(2)])

    def instance(i, a, b):
        return (i * 9 + 3 * (a + 1) + b + 1) * 2

    for r in range(z.source):
        for parity in range(2):
            work = []
            for a in (-1, 0, 1):
                i = r - 1 - a
                if not 0 <= i < z.dest:
                    continue
                for b in (-1, 0, 1):
                    slot = 3 * (a + 1) + b + 1
                    n = instance(i, a, b) + parity
                    other, shift = steps(b, offset[i][a + 1], parity)
                    row = table[2 * i + other, slot : slot + 1, :]
                    picks[n : n + 1, :] = lane_roll(row, shift, z.lanes)
                    work.append(n)
            for lane in range(0, z.lanes, LANES):
                at = slice(lane, lane + LANES)
                pick = [jnp.broadcast_to(picks[n : n + 1, at], (8, LANES)) for n in work]
                for k in range(z.bases):
                    mask = [p == float(k) for p in pick] if k else None
                    for v in range(0, z.vpad, 8):
                        value = product[2 * r + parity, k * z.vpad + v : k * z.vpad + v + 8, at]
                        if k == 0:
                            if v == 0:
                                best = {}
                            for m in range(len(work)):
                                best[m, v] = value
                        else:
                            for m in range(len(work)):
                                best[m, v] = jnp.where(mask[m], value, best[m, v])
                for m, n in enumerate(work):
                    for v in range(0, z.vpad, 8):
                        chosen[n, v : v + 8, at] = best[m, v]

    packed[...] = jnp.zeros_like(packed)
    for i in range(z.dest):
        for parity in range(2):
            total = None
            for a in (-1, 0, 1):
                for b in (-1, 0, 1):
                    other, shift = steps(-b, offset[i][a + 1], parity)
                    value = lane_roll(chosen[instance(i, a, b) + other], shift, z.lanes)
                    total = value if total is None else total + value
            block = 2 * i + parity
            if z.full:
                packed[block * z.full : (block + 1) * z.full] = total[0 : z.full]
            if z.rest:
                at = z.blocks * z.full + block * z.rest
                packed[at : at + z.rest] = total[z.full : z.variables]


def smoothed_derivative(difference):
    return difference * lax.rsqrt(difference * difference + smooth_square)


def backward_kernel(z, members, *refs):
    mine, others = refs[0], refs[1:members]
    own, one, two, picks, weight, step_table, out, obs, scale, grad, hi, lo, hi_odd, lo_odd = refs[members:]
    odd = lax.rem(lax.axis_index("lat"), 2)

    def table_rows(i, parity, start, count):
        at = parity * z.half + start
        if i == 0 or i == z.dest - 1:
            at += z.latent_rows
            a = one[at : at + count].astype(f32)
            b = two[at : at + count].astype(f32)
            return jnp.where(odd == 1, a, b) if i == 0 else jnp.where(odd == 1, b, a)
        at += z.latent_rows + (i - 1) * z.table
        return own[at : at + count].astype(f32)

    obs[...] = jnp.zeros_like(obs)
    scale[...] = jnp.zeros_like(scale)
    for i in range(z.dest):
        head = table_rows(i, 0, 0, z.pick_rows)
        cosine = head[z.slots + 3 : z.slots + 4] + head[z.slots + 4 : z.slots + 5]
        for parity in range(2):
            high = table_rows(i, parity, z.pick_rows, z.obs_rows)
            low = table_rows(i, parity, z.pick_rows + z.obs_rows, z.obs_rows)
            value = high + low
            block = 2 * i + parity
            if z.full:
                obs[block * z.full : (block + 1) * z.full] = value[0 : z.full]
                scale[block * z.full : (block + 1) * z.full] = jnp.broadcast_to(cosine, (z.full, z.lanes))
            if z.rest:
                at = z.blocks * z.full + block * z.rest
                obs[at : at + z.rest] = value[z.full : z.variables]
                scale[at : at + z.rest] = jnp.broadcast_to(cosine, (z.rest, z.lanes))
    value = mine[...]
    pairs = None
    for other in others:
        term = smoothed_derivative(value - other[...])
        pairs = term if pairs is None else pairs + term
    result = smoothed_derivative(value - obs[...])
    if pairs is not None:
        result = result - pairs * (1.0 / (members - 1))
    obs[...] = scale[...] * result
    grad[...] = jnp.zeros_like(grad)
    for block in range(z.blocks):
        if z.full:
            grad[block, 0 : z.full] = obs[block * z.full : (block + 1) * z.full]
        if z.rest:
            at = z.blocks * z.full + block * z.rest
            grad[block, z.full : z.variables] = obs[at : at + z.rest]

    for j in range(1, z.rows + 1):
        moved = {}
        for parity in range(2):
            for a in (-1, 0, 1):
                i = j - a
                for b in (-1, 0, 1):
                    other, shift = steps(b, step_table[3 * i + a + 1], parity)
                    moved[parity, a, b] = lane_roll(grad[2 * i + other], shift, z.lanes)
        for lane in range(0, z.lanes, LANES):
            at = slice(lane, lane + LANES)
            pick = {}
            for (parity, a, b) in moved:
                n = ((j - a) * 9 + 3 * (a + 1) + b + 1) * 2 + parity
                pick[parity, a, b] = jnp.broadcast_to(picks[n : n + 1, at], (8, LANES))
            for k in range(z.bases):
                total = {}
                for key, p in pick.items():
                    mask = p == float(k)
                    for v in range(0, z.vpad, 8):
                        term = jnp.where(mask, moved[key][v : v + 8, at], 0.0)
                        old = total.get((key[0], v))
                        total[key[0], v] = term if old is None else old + term
                for v in range(0, z.vpad, 16):
                    even = jnp.concatenate([total[0, v], total[0, v + 8]], axis=0)
                    half = 0.5 * jnp.concatenate([total[1, v], total[1, v + 8]], axis=0)
                    even = even + half
                    rows = slice((j - 1) * z.wrows + k * z.vpad + v, (j - 1) * z.wrows + k * z.vpad + v + 16)
                    top = even.astype(bf16)
                    hi[rows, at] = top
                    lo[rows, at] = (even - top.astype(f32)).astype(bf16)
                    top = half.astype(bf16)
                    hi_odd[rows, at] = top
                    lo_odd[rows, at] = (half - top.astype(f32)).astype(bf16)
    w = weight[...]
    contract = (((0,), (0,)), ((), ()))

    def multiply(x):
        return lax.dot_general(w, x, contract, preferred_element_type=f32)

    here = multiply(hi[...]) + multiply(lo[...])
    behind = multiply(hi_odd[...]) + multiply(lo_odd[...])
    field = here + pltpu.roll(behind, 1, axis=1)
    out[0] = field[0 : z.channels * z.rows, 0 : z.cols].reshape(z.channels, z.rows, z.cols)


def swaps(count, start):
    pairs = []
    for i in range(start, count - 1, 2):
        pairs += [(i, i + 1), (i + 1, i)]
    return pairs


def call(name, kernel, outs, scratch=(), out_specs=None, in_specs=None, inputs=()):
    size = sum(x.size * x.dtype.itemsize for x in tuple(inputs) + tuple(outs))
    return pl.pallas_call(
        kernel,
        name=name,
        out_shape=tuple(outs),
        in_specs=in_specs or [VMEM] * len(inputs),
        out_specs=out_specs or tuple([VMEM] * len(outs)),
        scratch_shapes=list(scratch),
        compiler_params=pltpu.CompilerParams(vmem_limit_bytes=VMEM_LIMIT),
        cost_estimate=pl.CostEstimate(flops=100_000_000, bytes_accessed=size, transcendentals=0),
    )(*inputs)


def on_device(hidden, filt, offsets, pick, observation, cosine):
    z = Sizes(hidden, filt)
    shape = jax.ShapeDtypeStruct
    own, edge = call(
        "prepare",
        functools.partial(prepare_kernel, z),
        [shape((z.own_rows, z.lanes), bf16), shape((z.own_rows, z.lanes - z.rim), bf16)],
        [pltpu.VMEM((z.half, 2 * z.lanes), f32)],
        inputs=(hidden, pick, observation, offsets.T, cosine[None]),
    )
    count = lax.axis_size("lon")
    right = lax.ppermute(edge, "lon", [((i + 1) % count, i) for i in range(count)])
    left = right
    if count != 2:
        left = lax.ppermute(edge, "lon", [(i, (i + 1) % count) for i in range(count)])
    whole, first, second = call(
        "merge",
        functools.partial(merge_kernel, z),
        [shape((z.own_rows, z.lanes), bf16)] + [shape((z.message, z.lanes), bf16)] * 2,
        inputs=(own, right, left),
    )
    count = lax.axis_size("lat")
    one = lax.ppermute(first, "lat", swaps(count, 0))
    two = lax.ppermute(second, "lat", swaps(count, 1))
    instances = z.dest * 9 * 2
    smem = pl.BlockSpec(memory_space=pltpu.SMEM)
    packed, picks, weight, step_table = call(
        "forward",
        functools.partial(forward_kernel, z),
        [
            shape((z.packed, z.lanes), f32),
            shape((instances, z.lanes), f32),
            shape((z.rows * z.wrows, z.latent_rows), bf16),
            shape((3 * z.dest,), jnp.int32),
        ],
        [
            pltpu.VMEM((2, z.message, z.lanes), bf16),
            pltpu.VMEM((z.blocks, z.pick_rows, z.lanes), f32),
            pltpu.VMEM((2 * z.source, z.wrows, z.lanes), f32),
            pltpu.VMEM((instances, z.vpad, z.lanes), f32),
            pltpu.VMEM((z.wrows, LANES), f32),
        ],
        out_specs=(VMEM, VMEM, VMEM, smem),
        inputs=(whole, one, two, filt),
    )
    members = lax.axis_size("ens")
    others = []
    for k in range(1, members):
        if members & (members - 1):
            route = [(i, (i + k) % members) for i in range(members)]
        else:
            route = [(i, i ^ k) for i in range(members)]
        others.append(lax.ppermute(packed, "ens", route))
    inputs = (packed, *others, whole, one, two, picks, weight, step_table)
    (result,) = call(
        "backward",
        functools.partial(backward_kernel, z, members),
        [shape(hidden.shape, f32)],
        [
            pltpu.VMEM((z.packed, z.lanes), f32),
            pltpu.VMEM((z.packed, z.lanes), f32),
            pltpu.VMEM((z.blocks, z.vpad, z.lanes), f32),
        ]
        + [pltpu.VMEM((z.rows * z.wrows, z.lanes), bf16)] * 4,
        in_specs=[VMEM] * (len(inputs) - 1) + [smem],
        inputs=inputs,
    )
    return result


def solution(mesh):
    return jax.shard_map(
        on_device,
        mesh=mesh,
        in_specs=(
            P("ens", None, "lat", "lon"),
            P(),
            P(None, "lat"),
            P(None, "lat", "lon"),
            P(None, "lat", "lon"),
            P("lat"),
        ),
        out_specs=P("ens", None, "lat", "lon"),
        check_vma=False,
    )
```

```python
import functools

import jax
import jax.numpy as jnp
from jax import lax
from jax.experimental import pallas as pl
from jax.experimental.pallas import tpu as pltpu
from jax.sharding import PartitionSpec as P

SPAN = 4
MARGIN = SPAN + 1
LANES = 128
SUB = 16
VMEM_LIMIT = 16 * 2**20

smooth_square = 0.01

f32 = jnp.float32
bf16 = jnp.bfloat16
VMEM = pl.BlockSpec(memory_space=pltpu.VMEM)
HBM = pl.BlockSpec(memory_space=pltpu.HBM)


def up_to(n, step):
    return -(-n // step) * step


class Sizes:
    def __init__(self, hidden, filt):
        _, self.channels, self.rows, self.cols = hidden.shape
        self.bases, self.variables, _ = filt.shape
        self.slots = 9
        self.lanes = up_to(self.cols + 2 * MARGIN, LANES)
        self.rim = (self.cols - MARGIN) // LANES * LANES
        self.paired = up_to(self.channels * self.rows, SUB)
        self.latent = up_to(self.channels, SUB)
        self.pick_rows = up_to(self.slots + 5, SUB)
        self.obs_rows = up_to(self.variables, SUB)
        self.half = self.pick_rows + 2 * self.obs_rows
        self.table = 2 * self.half
        self.table_at = self.rows * self.latent
        self.own_rows = self.table_at + self.rows * self.table
        self.dest = self.rows + 2
        self.vpad = up_to(self.variables, SUB)
        self.wrows = self.bases * self.vpad
        self.blocks = 2 * self.dest
        self.full = self.variables // 8 * 8
        self.rest = self.variables - self.full
        self.packed = up_to(self.blocks * self.variables, 8)
        self.value_rows = up_to(4 * self.variables, 8)
        self.head_at = self.latent
        self.value_at = self.head_at + SUB
        self.message = self.value_at + up_to(2 * self.value_rows, SUB)
        inner = range(1, self.rows + 1)
        self.inner = [(i, a) for i in inner for a in (-1, 0, 1) if i + a in inner]
        self.outer = [(0, 1), (self.dest - 1, -1), (1, -1), (self.rows, 1)]

    def block(self, n, count):
        ranges = []
        if self.full:
            ranges.append((slice(n * self.full, (n + 1) * self.full), slice(0, self.full)))
        if self.rest:
            at = count * self.full + n * self.rest
            ranges.append((slice(at, at + self.rest), slice(self.full, self.variables)))
        return ranges

    def own_table(self, i, parity, start):
        return self.table_at + (i - 1) * self.table + parity * self.half + start


def lane_roll(x, shift, lanes):
    if isinstance(shift, int):
        return x if shift % lanes == 0 else pltpu.roll(x, shift % lanes, axis=1)
    return pltpu.roll(x, jnp.where(shift < 0, shift + lanes, shift), axis=1)


def scalar_of(row):
    return jnp.max(row).astype(jnp.int32)


def steps(direction, offset, parity):
    if direction == 0:
        return parity, 0
    other = lax.rem(parity + offset, 2)
    return other, lax.shift_right_arithmetic(direction * offset + other - parity, 1)


def selection(shape, hit):
    row = lax.broadcasted_iota(jnp.int32, shape, 0)
    col = lax.broadcasted_iota(jnp.int32, shape, 1)
    return hit(row, col).astype(f32).astype(bf16)


def matmul(a, b):
    return jnp.dot(a, b, preferred_element_type=f32)


def is_odd_band():
    return lax.rem(lax.axis_index("lat"), 2) == 1


def prepare_kernel(z, *refs):
    arguments, (own, edge, work), local, arrived = refs[:5], refs[5:8], refs[8:13], refs[13]
    copies = []
    for n in range(5):
        copies.append(pltpu.make_async_copy(arguments[n], local[n], arrived.at[n]))
        copies[n].start()
    hidden, pick, obs, offsets, cosine = local
    wide = 2 * LANES
    split = selection(
        (wide, wide), lambda r, c: r == jnp.where(c < LANES, 2 * c, 2 * (c - LANES) + 1)
    )
    work[...] = jnp.zeros_like(work)
    for copy in copies[1:]:
        copy.wait()
    grid = 2 * z.cols
    for i in range(z.rows):
        work[0 : z.slots, 0:grid] = pick[:, i, :].astype(f32)
        o = obs[:, i, :]
        high = o.astype(bf16).astype(f32)
        work[z.pick_rows : z.pick_rows + z.variables, 0:grid] = high
        low_at = z.pick_rows + z.obs_rows
        work[low_at : low_at + z.variables, 0:grid] = o - high
        for t in range(3):
            work[z.slots + t : z.slots + t + 1, :] = jnp.broadcast_to(
                offsets[i : i + 1, t : t + 1].astype(f32), (1, work.shape[1])
            )
        c = cosine[0:1, i : i + 1]
        c_high = c.astype(bf16).astype(f32)
        work[z.slots + 3 : z.slots + 4, :] = jnp.broadcast_to(c_high, (1, work.shape[1]))
        work[z.slots + 4 : z.slots + 5, :] = jnp.broadcast_to(c - c_high, (1, work.shape[1]))
        at = z.table_at + i * z.table
        for n in range(z.lanes // LANES):
            parts = matmul(work[:, n * wide : (n + 1) * wide].astype(bf16), split).astype(bf16)
            for parity in range(2):
                own[at + parity * z.half : at + (parity + 1) * z.half, n * LANES : (n + 1) * LANES] = (
                    parts[:, parity * LANES : (parity + 1) * LANES]
                )
    copies[0].wait()
    pairs = z.channels * z.rows
    h = jnp.pad(
        hidden[0].reshape(pairs, z.cols), ((0, z.paired - pairs), (0, z.lanes - z.cols))
    )
    for i in range(z.rows):
        rows = selection((z.latent, z.paired), lambda r, c: c == r * z.rows + i)
        own[i * z.latent : (i + 1) * z.latent] = matmul(rows, h).astype(bf16)
    width = z.lanes - z.rim
    lane = lax.broadcasted_iota(jnp.int32, (z.own_rows, width), 1)
    first = pltpu.roll(own[:, 0:width].astype(f32), z.cols - z.rim, axis=1)
    last = pltpu.roll(own[:, z.rim :].astype(f32), z.lanes - z.cols, axis=1)
    ahead = (lane >= z.cols - z.rim) & (lane < z.cols - z.rim + MARGIN)
    behind = lane >= width - MARGIN
    edge[...] = jnp.where(ahead, first, jnp.where(behind, last, 0.0)).astype(bf16)


def weights_kernel(z, filt, narrow, paired, work):
    work[...] = jnp.zeros_like(work)
    for k in range(z.bases):
        work[k * z.vpad : k * z.vpad + z.variables, 0 : z.channels] = filt[k].astype(f32)
    flat = work[...].astype(bf16)
    narrow[...] = flat
    for i in range(z.rows):
        spread = selection((z.latent, z.paired), lambda r, c: c == r * z.rows + i)
        paired[i * z.wrows : (i + 1) * z.wrows] = matmul(flat, spread).astype(bf16)


def multiply(z, weight, latents, product, at):
    h = latents.astype(f32)
    halfway = (0.5 * (h + pltpu.roll(h, z.lanes - 1, axis=1))).astype(bf16)
    product[at] = matmul(weight, latents)
    product[at + 1] = matmul(weight, halfway)


def choose(z, product, at, work, picks, chosen):
    for lane in range(0, z.lanes, LANES):
        span = slice(lane, lane + LANES)
        pick = [jnp.broadcast_to(picks[n : n + 1, span], (8, LANES)) for n in work]
        best = {}
        for k in range(z.bases):
            mask = [p == float(k) for p in pick] if k else None
            for v in range(0, z.variables, 8):
                value = product[at, k * z.vpad + v : k * z.vpad + v + 8, span]
                for m in range(len(work)):
                    best[m, v] = jnp.where(mask[m], value, best[m, v]) if k else value
        for m, n in enumerate(work):
            for v in range(0, z.variables, 8):
                chosen[n, v : v + 8, span] = best[m, v]


def row_picks(z, pairs, offset, pick_row, picks):
    for at, (i, a) in enumerate(pairs):
        for b in (-1, 0, 1):
            for parity in range(2):
                other, shift = steps(b, offset(i, a), parity)
                n = (3 * at + b + 1) * 2 + parity
                picks[n : n + 1, :] = lane_roll(pick_row(i, a, b, other), shift, z.lanes)


def collect(z, pairs, offset, chosen, i, parity):
    total = None
    for at, (row, a) in enumerate(pairs):
        if row != i:
            continue
        for b in (-1, 0, 1):
            other, shift = steps(-b, offset(i, a), parity)
            value = lane_roll(chosen[(3 * at + b + 1) * 2 + other], shift, z.lanes)
            total = value if total is None else total + value
    return total


def own_kernel(z, own, right, left, weight, whole, one, two, product, partial, picks, table, chosen, values):
    whole[:, 0 : z.rim] = own[:, 0 : z.rim]
    width = z.lanes - z.rim
    lane = lax.broadcasted_iota(jnp.int32, (z.own_rows, width), 1)
    outer = jnp.where(lane >= width - MARGIN, left[...].astype(f32), right[...].astype(f32))
    inner = own[:, z.rim :].astype(f32)
    whole[:, z.rim :] = jnp.where(lane < z.cols - z.rim, inner, outer).astype(bf16)

    for i in range(1, z.rows + 1):
        for parity in range(2):
            at = z.own_table(i, parity, 0)
            table[2 * i - 2 + parity] = whole[at : at + z.pick_rows].astype(f32)
    offsets = {
        (i, a): scalar_of(table[2 * i - 2, z.slots + a + 1 : z.slots + a + 2, 0:LANES])
        for i, a in z.inner
    }

    def offset(i, a):
        return offsets[i, a]

    def pick_row(i, a, b, parity):
        slot = 3 * (a + 1) + b + 1
        return table[2 * i - 2 + parity, slot : slot + 1, :]

    row_picks(z, z.inner, offset, pick_row, picks)
    for s in range(1, z.rows + 1):
        multiply(z, weight[...], whole[(s - 1) * z.latent : s * z.latent], product, 2 * s - 2)
        for parity in range(2):
            work = [
                (3 * at + b) * 2 + parity
                for at, (i, a) in enumerate(z.inner)
                for b in range(3)
                if i + a == s
            ]
            choose(z, product, 2 * s - 2 + parity, work, picks, chosen)
    for i in range(1, z.rows + 1):
        for parity in range(2):
            partial[2 * i - 2 + parity] = collect(z, z.inner, offset, chosen, i, parity)

    odd = is_odd_band()

    def head(i, a):
        slot = 3 * (a + 1)
        return (
            [table[2 * i - 2 + parity, slot : slot + 3, :] for parity in range(2)]
            + [table[2 * i - 2, z.slots + a + 1 : z.slots + a + 2, :]]
            + [table[2 * i - 2, z.slots + 3 : z.slots + 5, :]]
        )

    def blocks(i):
        result = []
        for parity in range(2):
            at = z.own_table(i, parity, z.pick_rows)
            high = whole[at : at + z.obs_rows].astype(f32)
            low = whole[at + z.obs_rows : at + 2 * z.obs_rows].astype(f32)
            result.append(high + low)
        return result + [partial[2 * i - 2 + parity] for parity in range(2)]

    down, up = (z.rows, 1), (1, -1)
    heads = head(*down), head(*up)
    bodies = blocks(z.rows), blocks(1)
    for m, message in ((0, one), (1, two)):
        goes_up = odd if m == 0 else jnp.logical_not(odd)
        row = jnp.where(goes_up, 0, z.rows - 1)
        message[0 : z.latent] = whole[pl.ds(pl.multiple_of(row * z.latent, SUB), z.latent)]
        values[...] = jnp.zeros_like(values)
        at = 0
        for d, u in zip(*heads):
            values[at : at + d.shape[0]] = jnp.where(goes_up, u, d)
            at += d.shape[0]
        message[z.head_at : z.value_at] = values[0:SUB].astype(bf16)
        values[0:SUB] = jnp.zeros_like(values[0:SUB])
        for n, (d, u) in enumerate(zip(*bodies)):
            value = jnp.where(goes_up, u, d)
            high = value.astype(bf16).astype(f32)
            for packed_rows, rows in z.block(n, 4):
                values[packed_rows] = high[rows]
                low_rows = slice(packed_rows.start + z.value_rows, packed_rows.stop + z.value_rows)
                values[low_rows] = (value - high)[rows]
        message[z.value_at :] = values[...].astype(bf16)


def near_values(z, one, two, start, count):
    odd = is_odd_band()
    a, b = one[start : start + count].astype(f32), two[start : start + count].astype(f32)
    return jnp.where(odd, a, b), jnp.where(odd, b, a)


def near_block(z, values, n):
    result = []
    for packed_rows, rows in z.block(n, 4):
        low_rows = slice(packed_rows.start + z.value_rows, packed_rows.stop + z.value_rows)
        result.append((rows, values[packed_rows] + values[low_rows]))
    return result


def forward_kernel(z, whole, one, two, weight, own_product, partial, packed, picks, offset_rows, table, product, chosen):
    heads = near_values(z, one, two, z.head_at, SUB)
    for i in range(1, z.rows + 1):
        for parity in range(2):
            at = z.own_table(i, parity, 0)
            table[2 * i + parity] = whole[at : at + z.pick_rows].astype(f32)
    offset_rows[...] = jnp.zeros_like(offset_rows)
    for i in range(1, z.rows + 1):
        for t in range(3):
            offset_rows[3 * i + t : 3 * i + t + 1] = table[2 * i, z.slots + t : z.slots + t + 1, 0:LANES]
    for n, (i, a) in ((0, (0, 1)), (1, (z.dest - 1, -1))):
        slot = 3 * (a + 1)
        for parity in range(2):
            table[2 * i + parity, slot : slot + 3] = heads[n][3 * parity : 3 * parity + 3]
        offset_rows[3 * i + a + 1 : 3 * i + a + 2] = heads[n][6:7, 0:LANES]
    offsets = {
        (i, a): scalar_of(offset_rows[3 * i + a + 1 : 3 * i + a + 2]) for i, a in z.outer
    }

    def offset(i, a):
        return offsets[i, a]

    def pick_row(i, a, b, parity):
        slot = 3 * (a + 1) + b + 1
        return table[2 * i + parity, slot : slot + 1, :]

    row_picks(z, z.outer, offset, pick_row, picks)
    latents = near_values(z, one, two, 0, z.latent)
    for n in range(2):
        multiply(z, weight[...], latents[n].astype(bf16), product, 2 * n)
    for at, (i, a) in enumerate(z.outer):
        s = i + a
        for parity in range(2):
            work = [(3 * at + b) * 2 + parity for b in range(3)]
            if s in (0, z.dest - 1):
                choose(z, product, (2 if s else 0) + parity, work, picks, chosen)
            else:
                choose(z, own_product, 2 * s - 2 + parity, work, picks, chosen)
    if z.packed != z.blocks * z.variables:
        packed[...] = jnp.zeros_like(packed)
    bodies = near_values(z, one, two, z.value_at, 2 * z.value_rows)
    for i in range(z.dest):
        for parity in range(2):
            total = collect(z, z.outer, offset, chosen, i, parity)
            if 0 < i < z.dest - 1:
                before = partial[2 * i - 2 + parity]
                total = before if total is None else before + total
                for packed_rows, rows in z.block(2 * i + parity, z.blocks):
                    packed[packed_rows] = total[rows]
            else:
                before = near_block(z, bodies[1 if i else 0], 2 + parity)
                for (packed_rows, rows), (_, value) in zip(z.block(2 * i + parity, z.blocks), before):
                    packed[packed_rows] = total[rows] + value


def smoothed_derivative(difference):
    return difference * lax.rsqrt(difference * difference + smooth_square)


def observation_kernel(z, members, whole, one, two, packed, base, scale):
    if z.packed != z.blocks * z.variables:
        base[...] = jnp.zeros_like(base)
        scale[...] = jnp.zeros_like(scale)
    heads = near_values(z, one, two, z.head_at, SUB)
    bodies = near_values(z, one, two, z.value_at, 2 * z.value_rows)
    for i in range(z.dest):
        if 0 < i < z.dest - 1:
            at = z.own_table(i, 0, 0)
            first = whole[at : at + z.pick_rows].astype(f32)
            cosine = first[z.slots + 3 : z.slots + 4] + first[z.slots + 4 : z.slots + 5]
        else:
            first = heads[1 if i else 0]
            cosine = first[7:8] + first[8:9]
        for parity in range(2):
            if 0 < i < z.dest - 1:
                at = z.own_table(i, parity, z.pick_rows)
                high = whole[at : at + z.obs_rows].astype(f32)
                low = whole[at + z.obs_rows : at + 2 * z.obs_rows].astype(f32)
                seen = [(high + low)[rows] for _, rows in z.block(0, 1)]
            else:
                seen = [value for _, value in near_block(z, bodies[1 if i else 0], parity)]
            for (rows, _), value in zip(z.block(2 * i + parity, z.blocks), seen):
                weight = jnp.broadcast_to(cosine, value.shape)
                base[rows] = weight * smoothed_derivative(packed[rows] - value)
                scale[rows] = weight * (1.0 / max(members - 1, 1))


def backward_kernel(z, members, *refs):
    mine, others = refs[0], refs[1:members]
    base, scale, inner_picks, outer_picks, offset_rows, weight = refs[members : members + 6]
    out, flat, grad, even, odd, hi, lo = refs[members + 6 :]
    offset = {
        (i, a): scalar_of(offset_rows[3 * i + a + 1 : 3 * i + a + 2])
        for i, a in z.inner + z.outer[:2]
    }
    value = mine[...]
    pairs = jnp.zeros_like(value)
    for other in others:
        pairs = pairs + smoothed_derivative(value - other[...])
    flat[...] = base[...] - scale[...] * pairs
    grad[...] = jnp.zeros_like(grad)
    for block in range(z.blocks):
        for packed_rows, rows in z.block(block, z.blocks):
            grad[block, rows] = flat[packed_rows]

    for j in range(1, z.rows + 1):
        moved = {}
        for picks, sources in ((inner_picks, z.inner), (outer_picks, z.outer[:2])):
            for at, (i, a) in enumerate(sources):
                if i + a != j:
                    continue
                for b in (-1, 0, 1):
                    for parity in range(2):
                        other, shift = steps(b, offset[i, a], parity)
                        n = (3 * at + b + 1) * 2 + parity
                        moved[parity, i, b] = (
                            lane_roll(grad[2 * i + other], shift, z.lanes),
                            picks[n : n + 1, :],
                        )
        for lane in range(0, z.lanes, LANES):
            span = slice(lane, lane + LANES)
            for parity, part in ((0, even), (1, odd)):
                terms = [
                    (value[:, span], jnp.broadcast_to(pick[:, span], (8, LANES)))
                    for key, (value, pick) in moved.items()
                    if key[0] == parity
                ]
                for k in range(z.bases):
                    masks = [pick == float(k) for _, pick in terms]
                    for v in range(0, z.vpad, 8):
                        total = None
                        if v < z.variables:
                            for (value, _), mask in zip(terms, masks):
                                term = jnp.where(mask, value[v : v + 8], 0.0)
                                total = term if total is None else total + term
                        else:
                            total = jnp.zeros((8, LANES), f32)
                        part[k * z.vpad + v : k * z.vpad + v + 8, span] = total
        half = odd[...]
        total = even[...] + 0.5 * (half + pltpu.roll(half, 1, axis=1))
        top = total.astype(bf16)
        rows = slice((j - 1) * z.wrows, j * z.wrows)
        hi[rows] = top
        lo[rows] = (total - top.astype(f32)).astype(bf16)
    w = weight[...]
    contract = (((0,), (0,)), ((), ()))
    field = lax.dot_general(w, hi[...], contract, preferred_element_type=f32)
    field = field + lax.dot_general(w, lo[...], contract, preferred_element_type=f32)
    pairs = z.channels * z.rows
    out[0] = field[0:pairs, 0 : z.cols].reshape(z.channels, z.rows, z.cols)


def swaps(count, start):
    pairs = []
    for i in range(start, count - 1, 2):
        pairs += [(i, i + 1), (i + 1, i)]
    return pairs


def call(name, kernel, outs, inputs, scratch=(), in_specs=None, flops=10_000_000):
    size = sum(x.size * x.dtype.itemsize for x in tuple(inputs) + tuple(outs))
    return pl.pallas_call(
        kernel,
        name=name,
        out_shape=tuple(outs),
        in_specs=in_specs or [VMEM] * len(inputs),
        out_specs=tuple([VMEM] * len(outs)),
        scratch_shapes=list(scratch),
        compiler_params=pltpu.CompilerParams(vmem_limit_bytes=VMEM_LIMIT),
        cost_estimate=pl.CostEstimate(flops=flops, bytes_accessed=size, transcendentals=0),
    )(*inputs)


def on_device(hidden, filt, offsets, pick, observation, cosine):
    z = Sizes(hidden, filt)
    shape = jax.ShapeDtypeStruct
    arguments = (hidden, pick, observation, offsets.T, cosine[None])
    arguments = tuple(pltpu.with_memory_space_constraint(x, pltpu.HBM) for x in arguments)
    own, edge = call(
        "prepare",
        functools.partial(prepare_kernel, z),
        [shape((z.own_rows, z.lanes), bf16), shape((z.own_rows, z.lanes - z.rim), bf16)],
        arguments,
        [pltpu.VMEM((z.half, 2 * z.lanes), f32)]
        + [pltpu.VMEM(x.shape, x.dtype) for x in arguments]
        + [pltpu.SemaphoreType.DMA((5,))],
        in_specs=[HBM] * 5,
    )
    narrow, paired = call(
        "weights",
        functools.partial(weights_kernel, z),
        [shape((z.wrows, z.latent), bf16), shape((z.rows * z.wrows, z.paired), bf16)],
        (filt,),
        [pltpu.VMEM((z.wrows, z.latent), f32)],
    )
    count = lax.axis_size("lon")
    right = lax.ppermute(edge, "lon", [((i + 1) % count, i) for i in range(count)])
    left = right
    if count != 2:
        left = lax.ppermute(edge, "lon", [(i, (i + 1) % count) for i in range(count)])
    inner, outer = 6 * len(z.inner), 6 * len(z.outer)
    whole, first, second, product, partial, inner_picks = call(
        "own",
        functools.partial(own_kernel, z),
        [shape((z.own_rows, z.lanes), bf16)]
        + [shape((z.message, z.lanes), bf16)] * 2
        + [shape((2 * z.rows, z.wrows, z.lanes), f32)]
        + [shape((2 * z.rows, z.vpad, z.lanes), f32)]
        + [shape((inner, z.lanes), f32)],
        (own, right, left, narrow),
        [
            pltpu.VMEM((2 * z.rows, z.pick_rows, z.lanes), f32),
            pltpu.VMEM((inner, z.vpad, z.lanes), f32),
            pltpu.VMEM((z.message - z.value_at, z.lanes), f32),
        ],
    )
    count = lax.axis_size("lat")
    one = lax.ppermute(first, "lat", swaps(count, 0))
    two = lax.ppermute(second, "lat", swaps(count, 1))
    packed, outer_picks, offset_rows = call(
        "forward",
        functools.partial(forward_kernel, z),
        [
            shape((z.packed, z.lanes), f32),
            shape((outer, z.lanes), f32),
            shape((up_to(3 * z.dest, 8), LANES), f32),
        ],
        (whole, one, two, narrow, product, partial),
        [
            pltpu.VMEM((z.blocks, z.pick_rows, z.lanes), f32),
            pltpu.VMEM((4, z.wrows, z.lanes), f32),
            pltpu.VMEM((outer, z.vpad, z.lanes), f32),
        ],
    )
    members = lax.axis_size("ens")
    others = []
    for k in range(1, members):
        if members & (members - 1):
            route = [(i, (i + k) % members) for i in range(members)]
        else:
            route = [(i, i ^ k) for i in range(members)]
        others.append(lax.ppermute(packed, "ens", route))
    base, scale = call(
        "observe",
        functools.partial(observation_kernel, z, members),
        [shape((z.packed, z.lanes), f32)] * 2,
        (whole, one, two, packed),
    )
    (result,) = call(
        "backward",
        functools.partial(backward_kernel, z, members),
        [shape(hidden.shape, f32)],
        (packed, *others, base, scale, inner_picks, outer_picks, offset_rows, paired),
        [
            pltpu.VMEM((z.packed, z.lanes), f32),
            pltpu.VMEM((z.blocks, z.vpad, z.lanes), f32),
            pltpu.VMEM((z.wrows, z.lanes), f32),
            pltpu.VMEM((z.wrows, z.lanes), f32),
            pltpu.VMEM((z.rows * z.wrows, z.lanes), bf16),
            pltpu.VMEM((z.rows * z.wrows, z.lanes), bf16),
        ],
    )
    return result


def solution(mesh):
    return jax.shard_map(
        on_device,
        mesh=mesh,
        in_specs=(
            P("ens", None, "lat", "lon"),
            P(),
            P(None, "lat"),
            P(None, "lat", "lon"),
            P(None, "lat", "lon"),
            P("lat"),
        ),
        out_specs=P("ens", None, "lat", "lon"),
        check_vma=False,
    )
```

```python
import functools

import jax
import jax.numpy as jnp
from jax import lax
from jax.experimental import pallas as pl
from jax.experimental.pallas import tpu as pltpu
from jax.sharding import PartitionSpec as P

SPAN = 4
MARGIN = SPAN + 1
LANES = 128
SUB = 16
VMEM_LIMIT = 16 * 2**20

smooth_square = 0.01

f32 = jnp.float32
bf16 = jnp.bfloat16
VMEM = pl.BlockSpec(memory_space=pltpu.VMEM)
HBM = pl.BlockSpec(memory_space=pltpu.HBM)


def up_to(n, step):
    return -(-n // step) * step


class Sizes:
    def __init__(self, hidden, filt):
        _, self.channels, self.rows, self.cols = hidden.shape
        self.bases, self.variables, _ = filt.shape
        self.slots = 9
        self.lanes = up_to(self.cols + 2 * MARGIN, LANES)
        self.rim = (self.cols - MARGIN) // LANES * LANES
        self.paired = up_to(self.channels * self.rows, SUB)
        self.latent = up_to(self.channels, SUB)
        self.pick_rows = up_to(self.slots + 5, SUB)
        self.obs_rows = up_to(self.variables, SUB)
        self.half = self.pick_rows + 2 * self.obs_rows
        self.table = 2 * self.half
        self.table_at = self.rows * self.latent
        self.own_rows = self.table_at + self.rows * self.table
        self.dest = self.rows + 2
        self.vpad = up_to(self.variables, SUB)
        self.wrows = self.bases * self.vpad
        self.blocks = 2 * self.dest
        self.full = self.variables // 8 * 8
        self.rest = self.variables - self.full
        self.packed = up_to(self.blocks * self.variables, 8)
        self.value_rows = up_to(4 * self.variables, 8)
        self.head_at = self.latent
        self.value_at = self.head_at + SUB
        self.message = self.value_at + up_to(2 * self.value_rows, SUB)
        inner = range(1, self.rows + 1)
        self.inner = [(i, a) for i in inner for a in (-1, 0, 1) if i + a in inner]
        self.outer = [(0, 1), (self.dest - 1, -1), (1, -1), (self.rows, 1)]

    def block(self, n, count):
        ranges = []
        if self.full:
            ranges.append((slice(n * self.full, (n + 1) * self.full), slice(0, self.full)))
        if self.rest:
            at = count * self.full + n * self.rest
            ranges.append((slice(at, at + self.rest), slice(self.full, self.variables)))
        return ranges

    def own_table(self, i, parity, start):
        return self.table_at + (i - 1) * self.table + parity * self.half + start


def lane_roll(x, shift, lanes):
    if isinstance(shift, int):
        return x if shift % lanes == 0 else pltpu.roll(x, shift % lanes, axis=1)
    return pltpu.roll(x, jnp.where(shift < 0, shift + lanes, shift), axis=1)


def scalar_of(row):
    return jnp.max(row).astype(jnp.int32)


def steps(direction, offset, parity):
    if direction == 0:
        return parity, 0
    other = lax.rem(parity + offset, 2)
    return other, lax.shift_right_arithmetic(direction * offset + other - parity, 1)


def selection(shape, hit):
    row = lax.broadcasted_iota(jnp.int32, shape, 0)
    col = lax.broadcasted_iota(jnp.int32, shape, 1)
    return hit(row, col).astype(f32).astype(bf16)


def matmul(a, b):
    return jnp.dot(a, b, preferred_element_type=f32)


def is_odd_band():
    return lax.rem(lax.axis_index("lat"), 2) == 1


def prepare_kernel(z, *refs):
    arguments, (own, edge, work), local, arrived = refs[:5], refs[5:8], refs[8:13], refs[13]
    copies = []
    for n in range(5):
        copies.append(pltpu.make_async_copy(arguments[n], local[n], arrived.at[n]))
        copies[n].start()
    hidden, pick, obs, offsets, cosine = local
    wide = 2 * LANES
    split = selection(
        (wide, wide), lambda r, c: r == jnp.where(c < LANES, 2 * c, 2 * (c - LANES) + 1)
    )
    work[...] = jnp.zeros_like(work)
    for copy in copies[1:]:
        copy.wait()
    grid = 2 * z.cols
    for i in range(z.rows):
        work[0 : z.slots, 0:grid] = pick[:, i, :].astype(f32)
        o = obs[:, i, :]
        high = o.astype(bf16).astype(f32)
        work[z.pick_rows : z.pick_rows + z.variables, 0:grid] = high
        low_at = z.pick_rows + z.obs_rows
        work[low_at : low_at + z.variables, 0:grid] = o - high
        for t in range(3):
            work[z.slots + t : z.slots + t + 1, :] = jnp.broadcast_to(
                offsets[i : i + 1, t : t + 1].astype(f32), (1, work.shape[1])
            )
        c = cosine[0:1, i : i + 1]
        c_high = c.astype(bf16).astype(f32)
        work[z.slots + 3 : z.slots + 4, :] = jnp.broadcast_to(c_high, (1, work.shape[1]))
        work[z.slots + 4 : z.slots + 5, :] = jnp.broadcast_to(c - c_high, (1, work.shape[1]))
        at = z.table_at + i * z.table
        for n in range(z.lanes // LANES):
            parts = matmul(work[:, n * wide : (n + 1) * wide].astype(bf16), split).astype(bf16)
            for parity in range(2):
                own[at + parity * z.half : at + (parity + 1) * z.half, n * LANES : (n + 1) * LANES] = (
                    parts[:, parity * LANES : (parity + 1) * LANES]
                )
    copies[0].wait()
    pairs = z.channels * z.rows
    h = jnp.pad(
        hidden[0].reshape(pairs, z.cols), ((0, z.paired - pairs), (0, z.lanes - z.cols))
    )
    for i in range(z.rows):
        rows = selection((z.latent, z.paired), lambda r, c: c == r * z.rows + i)
        own[i * z.latent : (i + 1) * z.latent] = matmul(rows, h).astype(bf16)
    width = z.lanes - z.rim
    lane = lax.broadcasted_iota(jnp.int32, (z.own_rows, width), 1)
    first = pltpu.roll(own[:, 0:width].astype(f32), z.cols - z.rim, axis=1)
    last = pltpu.roll(own[:, z.rim :].astype(f32), z.lanes - z.cols, axis=1)
    ahead = (lane >= z.cols - z.rim) & (lane < z.cols - z.rim + MARGIN)
    behind = lane >= width - MARGIN
    edge[...] = jnp.where(ahead, first, jnp.where(behind, last, 0.0)).astype(bf16)


def weights_kernel(z, filt, narrow, paired, work):
    work[...] = jnp.zeros_like(work)
    for k in range(z.bases):
        work[k * z.vpad : k * z.vpad + z.variables, 0 : z.channels] = filt[k].astype(f32)
    flat = work[...].astype(bf16)
    narrow[...] = flat
    for i in range(z.rows):
        spread = selection((z.latent, z.paired), lambda r, c: c == r * z.rows + i)
        paired[i * z.wrows : (i + 1) * z.wrows] = matmul(flat, spread).astype(bf16)


def multiply(z, weight, latents, product, at):
    h = latents.astype(f32)
    halfway = (0.5 * (h + pltpu.roll(h, z.lanes - 1, axis=1))).astype(bf16)
    product[at] = matmul(weight, latents)
    product[at + 1] = matmul(weight, halfway)


def choose(z, product, at, work, picks, chosen):
    for lane in range(0, z.lanes, LANES):
        span = slice(lane, lane + LANES)
        pick = [jnp.broadcast_to(picks[n : n + 1, span], (8, LANES)) for n in work]
        best = {}
        for k in range(z.bases):
            mask = [p == float(k) for p in pick] if k else None
            for v in range(0, z.variables, 8):
                value = product[at, k * z.vpad + v : k * z.vpad + v + 8, span]
                for m in range(len(work)):
                    best[m, v] = jnp.where(mask[m], value, best[m, v]) if k else value
        for m, n in enumerate(work):
            for v in range(0, z.variables, 8):
                chosen[n, v : v + 8, span] = best[m, v]


def row_picks(z, pairs, offset, pick_row, picks):
    for at, (i, a) in enumerate(pairs):
        for b in (-1, 0, 1):
            for parity in range(2):
                other, shift = steps(b, offset(i, a), parity)
                n = (3 * at + b + 1) * 2 + parity
                picks[n : n + 1, :] = lane_roll(pick_row(i, a, b, other), shift, z.lanes)


def collect(z, pairs, offset, chosen, i, parity):
    total = None
    for at, (row, a) in enumerate(pairs):
        if row != i:
            continue
        for b in (-1, 0, 1):
            other, shift = steps(-b, offset(i, a), parity)
            value = lane_roll(chosen[(3 * at + b + 1) * 2 + other], shift, z.lanes)
            total = value if total is None else total + value
    return total


def own_kernel(z, own, right, left, weight, whole, one, two, product, partial, picks, table, chosen, values):
    whole[:, 0 : z.rim] = own[:, 0 : z.rim]
    width = z.lanes - z.rim
    lane = lax.broadcasted_iota(jnp.int32, (z.own_rows, width), 1)
    outer = jnp.where(lane >= width - MARGIN, left[...].astype(f32), right[...].astype(f32))
    inner = own[:, z.rim :].astype(f32)
    whole[:, z.rim :] = jnp.where(lane < z.cols - z.rim, inner, outer).astype(bf16)

    for i in range(1, z.rows + 1):
        for parity in range(2):
            at = z.own_table(i, parity, 0)
            table[2 * i - 2 + parity] = whole[at : at + z.pick_rows].astype(f32)
    offsets = {
        (i, a): scalar_of(table[2 * i - 2, z.slots + a + 1 : z.slots + a + 2, 0:LANES])
        for i, a in z.inner
    }

    def offset(i, a):
        return offsets[i, a]

    def pick_row(i, a, b, parity):
        slot = 3 * (a + 1) + b + 1
        return table[2 * i - 2 + parity, slot : slot + 1, :]

    row_picks(z, z.inner, offset, pick_row, picks)
    for s in range(1, z.rows + 1):
        multiply(z, weight[...], whole[(s - 1) * z.latent : s * z.latent], product, 2 * s - 2)
        for parity in range(2):
            work = [
                (3 * at + b) * 2 + parity
                for at, (i, a) in enumerate(z.inner)
                for b in range(3)
                if i + a == s
            ]
            choose(z, product, 2 * s - 2 + parity, work, picks, chosen)
    for i in range(1, z.rows + 1):
        for parity in range(2):
            partial[2 * i - 2 + parity] = collect(z, z.inner, offset, chosen, i, parity)

    odd = is_odd_band()

    def head(i, a):
        slot = 3 * (a + 1)
        return (
            [table[2 * i - 2 + parity, slot : slot + 3, :] for parity in range(2)]
            + [table[2 * i - 2, z.slots + a + 1 : z.slots + a + 2, :]]
            + [table[2 * i - 2, z.slots + 3 : z.slots + 5, :]]
        )

    def blocks(i):
        result = []
        for parity in range(2):
            at = z.own_table(i, parity, z.pick_rows)
            high = whole[at : at + z.obs_rows].astype(f32)
            low = whole[at + z.obs_rows : at + 2 * z.obs_rows].astype(f32)
            result.append(high + low)
        return result + [partial[2 * i - 2 + parity] for parity in range(2)]

    down, up = (z.rows, 1), (1, -1)
    heads = head(*down), head(*up)
    bodies = blocks(z.rows), blocks(1)
    for m, message in ((0, one), (1, two)):
        goes_up = odd if m == 0 else jnp.logical_not(odd)
        row = jnp.where(goes_up, 0, z.rows - 1)
        message[0 : z.latent] = whole[pl.ds(pl.multiple_of(row * z.latent, SUB), z.latent)]
        values[...] = jnp.zeros_like(values)
        at = 0
        for d, u in zip(*heads):
            values[at : at + d.shape[0]] = jnp.where(goes_up, u, d)
            at += d.shape[0]
        message[z.head_at : z.value_at] = values[0:SUB].astype(bf16)
        values[0:SUB] = jnp.zeros_like(values[0:SUB])
        for n, (d, u) in enumerate(zip(*bodies)):
            value = jnp.where(goes_up, u, d)
            high = value.astype(bf16).astype(f32)
            for packed_rows, rows in z.block(n, 4):
                values[packed_rows] = high[rows]
                low_rows = slice(packed_rows.start + z.value_rows, packed_rows.stop + z.value_rows)
                values[low_rows] = (value - high)[rows]
        message[z.value_at :] = values[...].astype(bf16)


def near_values(z, one, two, start, count):
    odd = is_odd_band()
    band = lax.axis_index("lat")
    a, b = one[start : start + count].astype(f32), two[start : start + count].astype(f32)
    above, below = jnp.where(odd, a, b), jnp.where(odd, b, a)
    return (
        jnp.where(band > 0, above, 0.0),
        jnp.where(band < lax.axis_size("lat") - 1, below, 0.0),
    )


def near_block(z, values, n):
    result = []
    for packed_rows, rows in z.block(n, 4):
        low_rows = slice(packed_rows.start + z.value_rows, packed_rows.stop + z.value_rows)
        result.append((rows, values[packed_rows] + values[low_rows]))
    return result


def forward_kernel(z, whole, one, two, weight, own_product, partial, packed, picks, offset_rows, table, product, chosen):
    heads = near_values(z, one, two, z.head_at, SUB)
    for i in range(1, z.rows + 1):
        for parity in range(2):
            at = z.own_table(i, parity, 0)
            table[2 * i + parity] = whole[at : at + z.pick_rows].astype(f32)
    offset_rows[...] = jnp.zeros_like(offset_rows)
    for i in range(1, z.rows + 1):
        for t in range(3):
            offset_rows[3 * i + t : 3 * i + t + 1] = table[2 * i, z.slots + t : z.slots + t + 1, 0:LANES]
    for n, (i, a) in ((0, (0, 1)), (1, (z.dest - 1, -1))):
        slot = 3 * (a + 1)
        for parity in range(2):
            table[2 * i + parity, slot : slot + 3] = heads[n][3 * parity : 3 * parity + 3]
        offset_rows[3 * i + a + 1 : 3 * i + a + 2] = heads[n][6:7, 0:LANES]
    offsets = {
        (i, a): scalar_of(offset_rows[3 * i + a + 1 : 3 * i + a + 2]) for i, a in z.outer
    }

    def offset(i, a):
        return offsets[i, a]

    def pick_row(i, a, b, parity):
        slot = 3 * (a + 1) + b + 1
        return table[2 * i + parity, slot : slot + 1, :]

    row_picks(z, z.outer, offset, pick_row, picks)
    latents = near_values(z, one, two, 0, z.latent)
    for n in range(2):
        multiply(z, weight[...], latents[n].astype(bf16), product, 2 * n)
    for at, (i, a) in enumerate(z.outer):
        s = i + a
        for parity in range(2):
            work = [(3 * at + b) * 2 + parity for b in range(3)]
            if s in (0, z.dest - 1):
                choose(z, product, (2 if s else 0) + parity, work, picks, chosen)
            else:
                choose(z, own_product, 2 * s - 2 + parity, work, picks, chosen)
    if z.packed != z.blocks * z.variables:
        packed[...] = jnp.zeros_like(packed)
    bodies = near_values(z, one, two, z.value_at, 2 * z.value_rows)
    for i in range(z.dest):
        for parity in range(2):
            total = collect(z, z.outer, offset, chosen, i, parity)
            if 0 < i < z.dest - 1:
                before = partial[2 * i - 2 + parity]
                total = before if total is None else before + total
                for packed_rows, rows in z.block(2 * i + parity, z.blocks):
                    packed[packed_rows] = total[rows]
            else:
                before = near_block(z, bodies[1 if i else 0], 2 + parity)
                for (packed_rows, rows), (_, value) in zip(z.block(2 * i + parity, z.blocks), before):
                    packed[packed_rows] = total[rows] + value


def smoothed_derivative(difference):
    return difference * lax.rsqrt(difference * difference + smooth_square)


def observation_kernel(z, members, whole, one, two, packed, base, scale):
    if z.packed != z.blocks * z.variables:
        base[...] = jnp.zeros_like(base)
        scale[...] = jnp.zeros_like(scale)
    heads = near_values(z, one, two, z.head_at, SUB)
    bodies = near_values(z, one, two, z.value_at, 2 * z.value_rows)
    for i in range(z.dest):
        if 0 < i < z.dest - 1:
            at = z.own_table(i, 0, 0)
            first = whole[at : at + z.pick_rows].astype(f32)
            cosine = first[z.slots + 3 : z.slots + 4] + first[z.slots + 4 : z.slots + 5]
        else:
            first = heads[1 if i else 0]
            cosine = first[7:8] + first[8:9]
        for parity in range(2):
            if 0 < i < z.dest - 1:
                at = z.own_table(i, parity, z.pick_rows)
                high = whole[at : at + z.obs_rows].astype(f32)
                low = whole[at + z.obs_rows : at + 2 * z.obs_rows].astype(f32)
                seen = [(high + low)[rows] for _, rows in z.block(0, 1)]
            else:
                seen = [value for _, value in near_block(z, bodies[1 if i else 0], parity)]
            for (rows, _), value in zip(z.block(2 * i + parity, z.blocks), seen):
                weight = jnp.broadcast_to(cosine, value.shape)
                base[rows] = weight * smoothed_derivative(packed[rows] - value)
                scale[rows] = weight * (1.0 / max(members - 1, 1))


def backward_kernel(z, members, *refs):
    mine, others = refs[0], refs[1:members]
    base, scale, inner_picks, outer_picks, offset_rows, weight = refs[members : members + 6]
    out, flat, grad, even, odd, hi, lo = refs[members + 6 :]
    offset = {
        (i, a): scalar_of(offset_rows[3 * i + a + 1 : 3 * i + a + 2])
        for i, a in z.inner + z.outer[:2]
    }
    value = mine[...]
    pairs = jnp.zeros_like(value)
    for other in others:
        pairs = pairs + smoothed_derivative(value - other[...])
    flat[...] = base[...] - scale[...] * pairs
    grad[...] = jnp.zeros_like(grad)
    for block in range(z.blocks):
        for packed_rows, rows in z.block(block, z.blocks):
            grad[block, rows] = flat[packed_rows]

    for j in range(1, z.rows + 1):
        moved = {}
        for picks, sources in ((inner_picks, z.inner), (outer_picks, z.outer[:2])):
            for at, (i, a) in enumerate(sources):
                if i + a != j:
                    continue
                for b in (-1, 0, 1):
                    for parity in range(2):
                        other, shift = steps(b, offset[i, a], parity)
                        n = (3 * at + b + 1) * 2 + parity
                        moved[parity, i, b] = (
                            lane_roll(grad[2 * i + other], shift, z.lanes),
                            picks[n : n + 1, :],
                        )
        for lane in range(0, z.lanes, LANES):
            span = slice(lane, lane + LANES)
            for parity, part in ((0, even), (1, odd)):
                terms = [
                    (value[:, span], jnp.broadcast_to(pick[:, span], (8, LANES)))
                    for key, (value, pick) in moved.items()
                    if key[0] == parity
                ]
                for k in range(z.bases):
                    masks = [pick == float(k) for _, pick in terms]
                    for v in range(0, z.vpad, 8):
                        total = None
                        if v < z.variables:
                            for (value, _), mask in zip(terms, masks):
                                term = jnp.where(mask, value[v : v + 8], 0.0)
                                total = term if total is None else total + term
                        else:
                            total = jnp.zeros((8, LANES), f32)
                        part[k * z.vpad + v : k * z.vpad + v + 8, span] = total
        half = odd[...]
        total = even[...] + 0.5 * (half + pltpu.roll(half, 1, axis=1))
        top = total.astype(bf16)
        rows = slice((j - 1) * z.wrows, j * z.wrows)
        hi[rows] = top
        lo[rows] = (total - top.astype(f32)).astype(bf16)
    w = weight[...]
    contract = (((0,), (0,)), ((), ()))
    field = lax.dot_general(w, hi[...], contract, preferred_element_type=f32)
    field = field + lax.dot_general(w, lo[...], contract, preferred_element_type=f32)
    pairs = z.channels * z.rows
    out[0] = field[0:pairs, 0 : z.cols].reshape(z.channels, z.rows, z.cols)


def swaps(bands, sectors, start):
    pairs = []
    for i in range(bands):
        other = i + 1 if (i - start) % 2 == 0 else i - 1
        for j in range(sectors):
            if 0 <= other < bands:
                pairs.append((i * sectors + j, other * sectors + j))
            else:
                pairs.append((i * sectors + j, i * sectors + (j + 1) % sectors))
    return pairs


def call(name, kernel, outs, inputs, scratch=(), in_specs=None, flops=10_000_000):
    size = sum(x.size * x.dtype.itemsize for x in tuple(inputs) + tuple(outs))
    return pl.pallas_call(
        kernel,
        name=name,
        out_shape=tuple(outs),
        in_specs=in_specs or [VMEM] * len(inputs),
        out_specs=tuple([VMEM] * len(outs)),
        scratch_shapes=list(scratch),
        compiler_params=pltpu.CompilerParams(vmem_limit_bytes=VMEM_LIMIT),
        cost_estimate=pl.CostEstimate(flops=flops, bytes_accessed=size, transcendentals=0),
    )(*inputs)


def on_device(hidden, filt, offsets, pick, observation, cosine):
    z = Sizes(hidden, filt)
    shape = jax.ShapeDtypeStruct
    arguments = (hidden, pick, observation, offsets.T, cosine[None])
    arguments = tuple(pltpu.with_memory_space_constraint(x, pltpu.HBM) for x in arguments)
    own, edge = call(
        "prepare",
        functools.partial(prepare_kernel, z),
        [shape((z.own_rows, z.lanes), bf16), shape((z.own_rows, z.lanes - z.rim), bf16)],
        arguments,
        [pltpu.VMEM((z.half, 2 * z.lanes), f32)]
        + [pltpu.VMEM(x.shape, x.dtype) for x in arguments]
        + [pltpu.SemaphoreType.DMA((5,))],
        in_specs=[HBM] * 5,
    )
    narrow, paired = call(
        "weights",
        functools.partial(weights_kernel, z),
        [shape((z.wrows, z.latent), bf16), shape((z.rows * z.wrows, z.paired), bf16)],
        (filt,),
        [pltpu.VMEM((z.wrows, z.latent), f32)],
    )
    count = lax.axis_size("lon")
    right = lax.ppermute(edge, "lon", [((i + 1) % count, i) for i in range(count)])
    left = right
    if count != 2:
        left = lax.ppermute(edge, "lon", [(i, (i + 1) % count) for i in range(count)])
    inner, outer = 6 * len(z.inner), 6 * len(z.outer)
    whole, first, second, product, partial, inner_picks = call(
        "own",
        functools.partial(own_kernel, z),
        [shape((z.own_rows, z.lanes), bf16)]
        + [shape((z.message, z.lanes), bf16)] * 2
        + [shape((2 * z.rows, z.wrows, z.lanes), f32)]
        + [shape((2 * z.rows, z.vpad, z.lanes), f32)]
        + [shape((inner, z.lanes), f32)],
        (own, right, left, narrow),
        [
            pltpu.VMEM((2 * z.rows, z.pick_rows, z.lanes), f32),
            pltpu.VMEM((inner, z.vpad, z.lanes), f32),
            pltpu.VMEM((z.message - z.value_at, z.lanes), f32),
        ],
    )
    bands = lax.axis_size("lat")
    one = lax.ppermute(first, ("lat", "lon"), swaps(bands, count, 0))
    two = lax.ppermute(second, ("lat", "lon"), swaps(bands, count, 1))
    packed, outer_picks, offset_rows = call(
        "forward",
        functools.partial(forward_kernel, z),
        [
            shape((z.packed, z.lanes), f32),
            shape((outer, z.lanes), f32),
            shape((up_to(3 * z.dest, 8), LANES), f32),
        ],
        (whole, one, two, narrow, product, partial),
        [
            pltpu.VMEM((z.blocks, z.pick_rows, z.lanes), f32),
            pltpu.VMEM((4, z.wrows, z.lanes), f32),
            pltpu.VMEM((outer, z.vpad, z.lanes), f32),
        ],
    )
    members = lax.axis_size("ens")
    others = []
    for k in range(1, members):
        if members & (members - 1):
            route = [(i, (i + k) % members) for i in range(members)]
        else:
            route = [(i, i ^ k) for i in range(members)]
        others.append(lax.ppermute(packed, "ens", route))
    base, scale = call(
        "observe",
        functools.partial(observation_kernel, z, members),
        [shape((z.packed, z.lanes), f32)] * 2,
        (whole, one, two, packed),
    )
    (result,) = call(
        "backward",
        functools.partial(backward_kernel, z, members),
        [shape(hidden.shape, f32)],
        (packed, *others, base, scale, inner_picks, outer_picks, offset_rows, paired),
        [
            pltpu.VMEM((z.packed, z.lanes), f32),
            pltpu.VMEM((z.blocks, z.vpad, z.lanes), f32),
            pltpu.VMEM((z.wrows, z.lanes), f32),
            pltpu.VMEM((z.wrows, z.lanes), f32),
            pltpu.VMEM((z.rows * z.wrows, z.lanes), bf16),
            pltpu.VMEM((z.rows * z.wrows, z.lanes), bf16),
        ],
    )
    return result


def solution(mesh):
    return jax.shard_map(
        on_device,
        mesh=mesh,
        in_specs=(
            P("ens", None, "lat", "lon"),
            P(),
            P(None, "lat"),
            P(None, "lat", "lon"),
            P(None, "lat", "lon"),
            P("lat"),
        ),
        out_specs=P("ens", None, "lat", "lon"),
        check_vma=False,
    )
```

```python
import functools

import jax
import jax.numpy as jnp
from jax import lax
from jax.experimental import pallas as pl
from jax.experimental.pallas import tpu as pltpu
from jax.sharding import PartitionSpec as P

SPAN = 4
MARGIN = SPAN + 1
REACH = (SPAN + 1) // 2
LANES = 128
SUB = 16
VMEM_LIMIT = 16 * 2**20

smooth_square = 0.01

f32 = jnp.float32
bf16 = jnp.bfloat16
VMEM = pl.BlockSpec(memory_space=pltpu.VMEM)
HBM = pl.BlockSpec(memory_space=pltpu.HBM)


def up_to(n, step):
    return -(-n // step) * step


class Sizes:
    def __init__(self, hidden, filt):
        _, self.channels, self.rows, self.cols = hidden.shape
        self.bases, self.variables, _ = filt.shape
        self.slots = 9
        self.lanes = up_to(self.cols + 2 * MARGIN, LANES)
        self.rim = (self.cols - MARGIN) // LANES * LANES
        self.paired = up_to(self.channels * self.rows, SUB)
        self.latent = up_to(self.channels, SUB)
        self.latents = self.paired
        self.pick_rows = up_to(self.slots + 5, SUB)
        self.obs_rows = up_to(self.variables, SUB)
        self.half = self.pick_rows + 2 * self.obs_rows
        self.table = 2 * self.half
        self.table_at = self.paired
        self.own_rows = self.table_at + self.rows * self.table
        self.dest = self.rows + 2
        self.vpad = up_to(self.variables, SUB)
        self.wrows = self.bases * self.vpad
        self.blocks = 2 * self.dest
        self.full = self.variables // 8 * 8
        self.rest = self.variables - self.full
        self.packed = up_to(self.blocks * self.variables, 8)
        self.value_rows = up_to(4 * self.variables, 8)
        self.head_at = self.latent
        self.value_at = self.head_at + SUB
        self.message = self.value_at + up_to(2 * self.value_rows, SUB)
        self.shared = up_to(2 * self.rows * self.rest, 8)
        self.shared_at = self.rows * self.bases * self.full
        self.depth = up_to(self.shared_at + self.bases * self.shared, SUB)
        inner = range(1, self.rows + 1)
        self.inner = [(i, a) for i in inner for a in (-1, 0, 1) if i + a in inner]
        self.outer = [(0, 1), (self.dest - 1, -1), (1, -1), (self.rows, 1)]

    def block(self, n, count):
        ranges = []
        if self.full:
            ranges.append((slice(n * self.full, (n + 1) * self.full), slice(0, self.full)))
        if self.rest:
            at = count * self.full + n * self.rest
            ranges.append((slice(at, at + self.rest), slice(self.full, self.variables)))
        return ranges

    def own_table(self, i, parity, start):
        return self.table_at + (i - 1) * self.table + parity * self.half + start


def lane_step(z, x, step):
    parts = [pltpu.roll(x[:, at : at + LANES], step, axis=1) for at in range(0, z.lanes, LANES)]
    first = lax.broadcasted_iota(jnp.int32, parts[0].shape, 1) < step
    return jnp.concatenate(
        [jnp.where(first, parts[n - 1], part) for n, part in enumerate(parts)], axis=1
    )


def moved_back(z, x):
    return pltpu.roll(x, z.lanes - REACH, axis=1)


def scalar_of(row):
    return jnp.max(row).astype(jnp.int32)


def steps(direction, offset, parity):
    other = lax.rem(parity + offset, 2)
    return other, REACH + lax.shift_right_arithmetic(direction * offset + other - parity, 1)


def selection(shape, hit):
    row = lax.broadcasted_iota(jnp.int32, shape, 0)
    col = lax.broadcasted_iota(jnp.int32, shape, 1)
    return hit(row, col).astype(f32).astype(bf16)


def matmul(a, b):
    return jnp.dot(a, b, preferred_element_type=f32)


def is_odd_band():
    return lax.rem(lax.axis_index("lat"), 2) == 1


def prepare_kernel(z, *refs):
    arguments, (own, edge, work), local, arrived = refs[:5], refs[5:8], refs[8:13], refs[13]
    copies = []
    for n in range(5):
        copies.append(pltpu.make_async_copy(arguments[n], local[n], arrived.at[n]))
        copies[n].start()
    hidden, pick, obs, offsets, cosine = local
    wide = 2 * LANES
    split = selection(
        (wide, wide), lambda r, c: r == jnp.where(c < LANES, 2 * c, 2 * (c - LANES) + 1)
    )
    work[...] = jnp.zeros_like(work)
    for copy in copies[1:]:
        copy.wait()
    grid = 2 * z.cols
    for i in range(z.rows):
        work[0 : z.slots, 0:grid] = pick[:, i, :].astype(f32)
        o = obs[:, i, :]
        high = o.astype(bf16).astype(f32)
        work[z.pick_rows : z.pick_rows + z.variables, 0:grid] = high
        low_at = z.pick_rows + z.obs_rows
        work[low_at : low_at + z.variables, 0:grid] = o - high
        for t in range(3):
            work[z.slots + t : z.slots + t + 1, :] = jnp.broadcast_to(
                offsets[i : i + 1, t : t + 1].astype(f32), (1, work.shape[1])
            )
        c = cosine[0:1, i : i + 1]
        c_high = c.astype(bf16).astype(f32)
        work[z.slots + 3 : z.slots + 4, :] = jnp.broadcast_to(c_high, (1, work.shape[1]))
        work[z.slots + 4 : z.slots + 5, :] = jnp.broadcast_to(c - c_high, (1, work.shape[1]))
        at = z.table_at + i * z.table
        for n in range(z.lanes // LANES):
            parts = matmul(work[:, n * wide : (n + 1) * wide].astype(bf16), split).astype(bf16)
            for parity in range(2):
                own[at + parity * z.half : at + (parity + 1) * z.half, n * LANES : (n + 1) * LANES] = (
                    parts[:, parity * LANES : (parity + 1) * LANES]
                )
    copies[0].wait()
    pairs = z.channels * z.rows
    own[0 : z.paired] = jnp.pad(
        hidden[0].reshape(pairs, z.cols), ((0, z.paired - pairs), (0, z.lanes - z.cols))
    )
    width = z.lanes - z.rim
    lane = lax.broadcasted_iota(jnp.int32, (z.own_rows, width), 1)
    first = pltpu.roll(own[:, 0:width].astype(f32), z.cols - z.rim, axis=1)
    last = pltpu.roll(own[:, z.rim :].astype(f32), z.lanes - z.cols, axis=1)
    ahead = (lane >= z.cols - z.rim) & (lane < z.cols - z.rim + MARGIN)
    behind = lane >= width - MARGIN
    edge[...] = jnp.where(ahead, first, jnp.where(behind, last, 0.0)).astype(bf16)


def weights_kernel(z, filt, narrow, paired, turned, work, spread_out):
    work[...] = jnp.zeros_like(work)
    for k in range(z.bases):
        work[k * z.vpad : k * z.vpad + z.variables, 0 : z.channels] = filt[k].astype(f32)
    flat = work[...].astype(bf16)
    narrow[...] = flat
    total = None
    for i in range(z.rows):
        spread = selection((z.latent, z.paired), lambda r, c: c == r * z.rows + i)
        paired[i * z.wrows : (i + 1) * z.wrows] = matmul(flat, spread).astype(bf16)
        spread_out[...] = jnp.zeros_like(spread_out)
        for k in range(z.bases):
            w = work[k * z.vpad : k * z.vpad + z.variables]
            if z.full:
                at = (i * z.bases + k) * z.full
                spread_out[at : at + z.full] = w[0 : z.full]
            for parity in range(2):
                if z.rest:
                    at = z.shared_at + k * z.shared + (2 * i + parity) * z.rest
                    spread_out[at : at + z.rest] = w[z.full :]
        turned_spread = selection((z.paired, z.latent), lambda r, c: r == c * z.rows + i)
        part = lax.dot_general(
            turned_spread,
            spread_out[...].astype(bf16),
            (((1,), (1,)), ((), ())),
            preferred_element_type=f32,
        )
        total = part if total is None else total + part
    turned[...] = total.astype(bf16)


def halfway(z, latents):
    h = latents.astype(f32)
    return (0.5 * (h + pltpu.roll(h, z.lanes - 1, axis=1))).astype(bf16)


def choose(z, product, at, work, picks, chosen):
    for lane in range(0, z.lanes, LANES):
        span = slice(lane, lane + LANES)
        pick = [jnp.broadcast_to(picks[n : n + 1, span], (8, LANES)) for n in work]
        best = {}
        for k in range(z.bases):
            mask = [p == float(k) for p in pick] if k else None
            for v in range(0, z.variables, 8):
                value = product[at, k * z.vpad + v : k * z.vpad + v + 8, span]
                for m in range(len(work)):
                    best[m, v] = jnp.where(mask[m], value, best[m, v]) if k else value
        for m, n in enumerate(work):
            for v in range(0, z.variables, 8):
                chosen[n, v : v + 8, span] = best[m, v]


def row_picks(z, pairs, offset, pick_rows, picks):
    for at, (i, a) in enumerate(pairs):
        for b in (-1, 0, 1):
            for parity in range(2):
                n = (3 * at + b + 1) * 2 + parity
                if b == 0:
                    picks[n : n + 1, :] = pick_rows(i, a, b, parity, False)
                    continue
                other, step = steps(b, offset(i, a), parity)
                picks[n : n + 1, :] = lane_step(z, pick_rows(i, a, b, other, True), step)


def collect(z, pairs, offset, chosen, i, parity):
    here, aside = None, None
    for at, (row, a) in enumerate(pairs):
        if row != i:
            continue
        value = chosen[(3 * at + 1) * 2 + parity]
        here = value if here is None else here + value
        for b in (-1, 1):
            other, step = steps(-b, offset(i, a), parity)
            value = lane_step(z, chosen[(3 * at + b + 1) * 2 + other], step)
            aside = value if aside is None else aside + value
    return None if here is None else here + moved_back(z, aside)


def own_kernel(z, own, right, left, weight, whole, one, two, product, partial, picks, table, aside, chosen, values):
    whole[:, 0 : z.rim] = own[:, 0 : z.rim]
    width = z.lanes - z.rim
    lane = lax.broadcasted_iota(jnp.int32, (z.own_rows, width), 1)
    outer = jnp.where(lane >= width - MARGIN, left[...].astype(f32), right[...].astype(f32))
    inner = own[:, z.rim :].astype(f32)
    whole[:, z.rim :] = jnp.where(lane < z.cols - z.rim, inner, outer).astype(bf16)

    for i in range(1, z.rows + 1):
        for parity in range(2):
            at = z.own_table(i, parity, 0)
            rows = whole[at : at + z.pick_rows].astype(f32)
            table[2 * i - 2 + parity] = rows
            aside[2 * i - 2 + parity] = moved_back(z, rows)
    offsets = {
        (i, a): scalar_of(table[2 * i - 2, z.slots + a + 1 : z.slots + a + 2, 0:LANES])
        for i, a in z.inner
    }

    def offset(i, a):
        return offsets[i, a]

    def pick_rows(i, a, b, parity, back):
        slot = 3 * (a + 1) + b + 1
        return (aside if back else table)[2 * i - 2 + parity, slot : slot + 1, :]

    latents = whole[0 : z.paired]
    for parity, x in enumerate((latents, halfway(z, latents))):
        both = matmul(weight[...], x)
        for i in range(z.rows):
            product[2 * i + parity] = both[i * z.wrows : (i + 1) * z.wrows]
    row_picks(z, z.inner, offset, pick_rows, picks)
    for s in range(1, z.rows + 1):
        for parity in range(2):
            work = [
                (3 * at + b) * 2 + parity
                for at, (i, a) in enumerate(z.inner)
                for b in range(3)
                if i + a == s
            ]
            choose(z, product, 2 * s - 2 + parity, work, picks, chosen)
    for i in range(1, z.rows + 1):
        for parity in range(2):
            partial[2 * i - 2 + parity] = collect(z, z.inner, offset, chosen, i, parity)

    odd = is_odd_band()

    def head(i, a):
        slot = 3 * (a + 1)
        return (
            [table[2 * i - 2 + parity, slot : slot + 3, :] for parity in range(2)]
            + [table[2 * i - 2, z.slots + a + 1 : z.slots + a + 2, :]]
            + [table[2 * i - 2, z.slots + 3 : z.slots + 5, :]]
        )

    def blocks(i):
        result = []
        for parity in range(2):
            at = z.own_table(i, parity, z.pick_rows)
            high = whole[at : at + z.obs_rows].astype(f32)
            low = whole[at + z.obs_rows : at + 2 * z.obs_rows].astype(f32)
            result.append(high + low)
        return result + [partial[2 * i - 2 + parity] for parity in range(2)]

    down, up = (z.rows, 1), (1, -1)
    heads = head(*down), head(*up)
    bodies = blocks(z.rows), blocks(1)
    for m, message in ((0, one), (1, two)):
        goes_up = odd if m == 0 else jnp.logical_not(odd)
        row = jnp.where(goes_up, 0, z.rows - 1)
        boundary = selection((z.latent, z.paired), lambda r, c: c == r * z.rows + row)
        message[0 : z.latent] = matmul(boundary, latents).astype(bf16)
        values[...] = jnp.zeros_like(values)
        at = 0
        for d, u in zip(*heads):
            values[at : at + d.shape[0]] = jnp.where(goes_up, u, d)
            at += d.shape[0]
        message[z.head_at : z.value_at] = values[0:SUB].astype(bf16)
        values[0:SUB] = jnp.zeros_like(values[0:SUB])
        for n, (d, u) in enumerate(zip(*bodies)):
            value = jnp.where(goes_up, u, d)
            high = value.astype(bf16).astype(f32)
            for packed_rows, rows in z.block(n, 4):
                values[packed_rows] = high[rows]
                low_rows = slice(packed_rows.start + z.value_rows, packed_rows.stop + z.value_rows)
                values[low_rows] = (value - high)[rows]
        message[z.value_at :] = values[...].astype(bf16)


def near_values(z, one, two, start, count):
    odd = is_odd_band()
    band = lax.axis_index("lat")
    a, b = one[start : start + count].astype(f32), two[start : start + count].astype(f32)
    above, below = jnp.where(odd, a, b), jnp.where(odd, b, a)
    return (
        jnp.where(band > 0, above, 0.0),
        jnp.where(band < lax.axis_size("lat") - 1, below, 0.0),
    )


def near_block(z, values, n):
    result = []
    for packed_rows, rows in z.block(n, 4):
        low_rows = slice(packed_rows.start + z.value_rows, packed_rows.stop + z.value_rows)
        result.append((rows, values[packed_rows] + values[low_rows]))
    return result


def forward_kernel(z, whole, one, two, weight, own_product, partial, packed, picks, offset_rows, table, aside, product, chosen):
    heads = near_values(z, one, two, z.head_at, SUB)
    for i in range(1, z.rows + 1):
        for parity in range(2):
            at = z.own_table(i, parity, 0)
            table[2 * i + parity] = whole[at : at + z.pick_rows].astype(f32)
    offset_rows[...] = jnp.zeros_like(offset_rows)
    for i in range(1, z.rows + 1):
        for t in range(3):
            offset_rows[3 * i + t : 3 * i + t + 1] = table[2 * i, z.slots + t : z.slots + t + 1, 0:LANES]
    for n, (i, a) in ((0, (0, 1)), (1, (z.dest - 1, -1))):
        slot = 3 * (a + 1)
        for parity in range(2):
            table[2 * i + parity, slot : slot + 3] = heads[n][3 * parity : 3 * parity + 3]
        offset_rows[3 * i + a + 1 : 3 * i + a + 2] = heads[n][6:7, 0:LANES]
    for block in range(z.blocks):
        aside[block] = moved_back(z, table[block])
    offsets = {
        (i, a): scalar_of(offset_rows[3 * i + a + 1 : 3 * i + a + 2]) for i, a in z.outer
    }

    def offset(i, a):
        return offsets[i, a]

    def pick_rows(i, a, b, parity, back):
        slot = 3 * (a + 1) + b + 1
        return (aside if back else table)[2 * i + parity, slot : slot + 1, :]

    latents = near_values(z, one, two, 0, z.latent)
    for n in range(2):
        x = latents[n].astype(bf16)
        product[2 * n] = matmul(weight[...], x)
        product[2 * n + 1] = matmul(weight[...], halfway(z, x))
    row_picks(z, z.outer, offset, pick_rows, picks)
    for at, (i, a) in enumerate(z.outer):
        s = i + a
        for parity in range(2):
            work = [(3 * at + b) * 2 + parity for b in range(3)]
            if s in (0, z.dest - 1):
                choose(z, product, (2 if s else 0) + parity, work, picks, chosen)
            else:
                choose(z, own_product, 2 * s - 2 + parity, work, picks, chosen)
    if z.packed != z.blocks * z.variables:
        packed[...] = jnp.zeros_like(packed)
    bodies = near_values(z, one, two, z.value_at, 2 * z.value_rows)
    for i in range(z.dest):
        for parity in range(2):
            total = collect(z, z.outer, offset, chosen, i, parity)
            if 0 < i < z.dest - 1:
                before = partial[2 * i - 2 + parity]
                total = before if total is None else before + total
                for packed_rows, rows in z.block(2 * i + parity, z.blocks):
                    packed[packed_rows] = total[rows]
            else:
                before = near_block(z, bodies[1 if i else 0], 2 + parity)
                for (packed_rows, rows), (_, value) in zip(z.block(2 * i + parity, z.blocks), before):
                    packed[packed_rows] = total[rows] + value


def smoothed_derivative(difference):
    return difference * lax.rsqrt(difference * difference + smooth_square)


def observation_kernel(z, members, whole, one, two, packed, inner_picks, outer_picks, base, scale, shared):
    shared[...] = jnp.zeros_like(shared)
    for picks, i, a, n in gradient_sources(z, inner_picks, outer_picks):
        for b in (-1, 0, 1):
            for parity in range(2):
                row = picks[n + 2 * (b + 1) + parity : n + 2 * (b + 1) + parity + 1, :]
                if z.rest:
                    at = (2 * (i + a - 1) + parity) * z.rest
                    shared[3 * (a + 1) + b + 1, at : at + z.rest] = jnp.broadcast_to(row, (z.rest, z.lanes))
    if z.packed != z.blocks * z.variables:
        base[...] = jnp.zeros_like(base)
        scale[...] = jnp.zeros_like(scale)
    heads = near_values(z, one, two, z.head_at, SUB)
    bodies = near_values(z, one, two, z.value_at, 2 * z.value_rows)
    for i in range(z.dest):
        if 0 < i < z.dest - 1:
            at = z.own_table(i, 0, 0)
            first = whole[at : at + z.pick_rows].astype(f32)
            cosine = first[z.slots + 3 : z.slots + 4] + first[z.slots + 4 : z.slots + 5]
        else:
            first = heads[1 if i else 0]
            cosine = first[7:8] + first[8:9]
        for parity in range(2):
            if 0 < i < z.dest - 1:
                at = z.own_table(i, parity, z.pick_rows)
                high = whole[at : at + z.obs_rows].astype(f32)
                low = whole[at + z.obs_rows : at + 2 * z.obs_rows].astype(f32)
                seen = [(high + low)[rows] for _, rows in z.block(0, 1)]
            else:
                seen = [value for _, value in near_block(z, bodies[1 if i else 0], parity)]
            for (rows, _), value in zip(z.block(2 * i + parity, z.blocks), seen):
                weight = jnp.broadcast_to(cosine, value.shape)
                base[rows] = weight * smoothed_derivative(packed[rows] - value)
                scale[rows] = weight * (1.0 / max(members - 1, 1))


def gradient_sources(z, inner_picks, outer_picks):
    result = []
    for picks, pairs in ((inner_picks, z.inner), (outer_picks, z.outer[:2])):
        for at, (i, a) in enumerate(pairs):
            result.append((picks, i, a, 6 * at))
    return result


def backward_kernel(z, members, *refs):
    mine, others = refs[0], refs[1:members]
    base, scale, inner_picks, outer_picks, shared_picks, offset_rows, weight = refs[members : members + 7]
    out, flat, back, rest, rest_back, shared, even, odd, extra, hi, lo, stage, sent = refs[members + 7 :]
    sources = gradient_sources(z, inner_picks, outer_picks)
    offset = {
        (i, a): scalar_of(offset_rows[3 * i + a + 1 : 3 * i + a + 2]) for _, i, a, _ in sources
    }
    value = mine[...]
    pairs = jnp.zeros_like(value)
    for other in others:
        pairs = pairs + smoothed_derivative(value - other[...])
    gradient = base[...] - scale[...] * pairs
    flat[...] = gradient
    back[...] = moved_back(z, gradient)
    if z.rest:
        rest[...] = jnp.zeros_like(rest)
        rest_back[...] = jnp.zeros_like(rest_back)
        for block in range(z.blocks):
            at = z.blocks * z.full + block * z.rest
            rest[block, 0 : z.rest] = flat[at : at + z.rest]
            rest_back[block, 0 : z.rest] = back[at : at + z.rest]
        shared[...] = jnp.zeros_like(shared)

    moved, pick = {}, {}
    for picks, i, a, n in sources:
        j = i + a
        for b in (-1, 0, 1):
            for parity in range(2):
                key = j, parity, a, b
                at = n + 2 * (b + 1) + parity
                pick[key] = picks[at : at + 1, :]
                block = 2 * i + parity
                if b == 0:
                    if z.full:
                        moved[key] = flat[block * z.full : (block + 1) * z.full]
                    if z.rest:
                        tail = rest[block]
                else:
                    other, step = steps(b, offset[i, a], parity)
                    block = 2 * i + other
                    if z.full:
                        moved[key] = lane_step(
                            z, back[pl.ds(pl.multiple_of(block * z.full, 8), z.full)], step
                        )
                    if z.rest:
                        tail = lane_step(z, rest_back[block], step)
                if z.rest:
                    at = (2 * (j - 1) + parity) * z.rest
                    shared[3 * (a + 1) + b + 1, at : at + z.rest] = tail[0 : z.rest]

    def gather(terms, k):
        total = None
        for value, p in terms:
            term = jnp.where(p == float(k), value, 0.0)
            total = term if total is None else total + term
        return total

    def keep(rows, total):
        top = total.astype(bf16)
        hi[rows] = top
        lo[rows] = (total - top.astype(f32)).astype(bf16)

    hi[z.shared_at :] = jnp.zeros_like(hi[z.shared_at :])
    lo[z.shared_at :] = jnp.zeros_like(lo[z.shared_at :])
    if z.full:
        for j in range(1, z.rows + 1):
            for at in range(0, z.lanes, LANES):
                span = slice(at, at + LANES)
                for parity, part in ((0, even), (1, odd)):
                    keys = [key for key in pick if key[:2] == (j, parity)]
                    wide = [jnp.broadcast_to(pick[key][:, span], (8, LANES)) for key in keys]
                    for v in range(0, z.full, 8):
                        terms = [(moved[key][v : v + 8, span], p) for key, p in zip(keys, wide)]
                        for k in range(z.bases):
                            part[k * z.full + v : k * z.full + v + 8, span] = gather(terms, k)
            half = odd[...]
            total = even[...] + 0.5 * (half + pltpu.roll(half, 1, axis=1))
            at = (j - 1) * z.bases * z.full
            keep(slice(at, at + z.bases * z.full), total)
    if z.rest:
        for at in range(0, z.lanes, LANES):
            span = slice(at, at + LANES)
            for v in range(0, z.shared, 8):
                terms = [
                    (shared[slot, v : v + 8, span], shared_picks[slot, v : v + 8, span])
                    for slot in range(z.slots)
                ]
                for k in range(z.bases):
                    extra[k * z.shared + v : k * z.shared + v + 8, span] = gather(terms, k)
        total = extra[...]
        row = lax.rem(lax.broadcasted_iota(jnp.int32, total.shape, 0), z.shared)
        is_odd = lax.rem(lax.div(row, z.rest), 2) == 1
        total = jnp.where(is_odd, 0.5 * (total + pltpu.roll(total, 1, axis=1)), total)
        keep(slice(z.shared_at, z.shared_at + z.bases * z.shared), total)

    pieces = 3
    length = up_to(-(-z.channels // pieces), SUB // 2)
    copies = []
    for first in range(0, z.channels, length):
        last = min(first + length, z.channels)
        w = weight[first * z.rows : up_to(last * z.rows, SUB)]
        field = matmul(w, hi[...]) + matmul(w, lo[...])
        count = last - first
        stage[first:last] = field[0 : count * z.rows, 0 : z.cols].reshape(count, z.rows, z.cols)
        copy = pltpu.make_async_copy(
            stage.at[first:last], out.at[0, first:last], sent.at[len(copies)]
        )
        copy.start()
        copies.append(copy)
    for copy in copies:
        copy.wait()


def swaps(bands, sectors, start):
    pairs = []
    for i in range(bands):
        other = i + 1 if (i - start) % 2 == 0 else i - 1
        for j in range(sectors):
            if 0 <= other < bands:
                pairs.append((i * sectors + j, other * sectors + j))
            else:
                pairs.append((i * sectors + j, i * sectors + (j + 1) % sectors))
    return pairs


def call(name, kernel, outs, inputs, scratch=(), in_specs=None, out_specs=None, flops=10_000_000):
    size = sum(x.size * x.dtype.itemsize for x in tuple(inputs) + tuple(outs))
    return pl.pallas_call(
        kernel,
        name=name,
        out_shape=tuple(outs),
        in_specs=in_specs or [VMEM] * len(inputs),
        out_specs=out_specs or tuple([VMEM] * len(outs)),
        scratch_shapes=list(scratch),
        compiler_params=pltpu.CompilerParams(vmem_limit_bytes=VMEM_LIMIT),
        cost_estimate=pl.CostEstimate(flops=flops, bytes_accessed=size, transcendentals=0),
    )(*inputs)


def on_device(hidden, filt, offsets, pick, observation, cosine):
    z = Sizes(hidden, filt)
    shape = jax.ShapeDtypeStruct
    arguments = (hidden, pick, observation, offsets.T, cosine[None])
    arguments = tuple(pltpu.with_memory_space_constraint(x, pltpu.HBM) for x in arguments)
    own, edge = call(
        "prepare",
        functools.partial(prepare_kernel, z),
        [shape((z.own_rows, z.lanes), bf16), shape((z.own_rows, z.lanes - z.rim), bf16)],
        arguments,
        [pltpu.VMEM((z.half, 2 * z.lanes), f32)]
        + [pltpu.VMEM(x.shape, x.dtype) for x in arguments]
        + [pltpu.SemaphoreType.DMA((5,))],
        in_specs=[HBM] * 5,
    )
    narrow, paired, turned = call(
        "weights",
        functools.partial(weights_kernel, z),
        [
            shape((z.wrows, z.latent), bf16),
            shape((z.rows * z.wrows, z.paired), bf16),
            shape((z.paired, z.depth), bf16),
        ],
        (filt,),
        [pltpu.VMEM((z.wrows, z.latent), f32), pltpu.VMEM((z.depth, z.latent), f32)],
    )
    count = lax.axis_size("lon")
    right = lax.ppermute(edge, "lon", [((i + 1) % count, i) for i in range(count)])
    left = right
    if count != 2:
        left = lax.ppermute(edge, "lon", [(i, (i + 1) % count) for i in range(count)])
    inner, outer = 6 * len(z.inner), 6 * len(z.outer)
    whole, first, second, product, partial, inner_picks = call(
        "own",
        functools.partial(own_kernel, z),
        [shape((z.own_rows, z.lanes), bf16)]
        + [shape((z.message, z.lanes), bf16)] * 2
        + [shape((2 * z.rows, z.wrows, z.lanes), f32)]
        + [shape((2 * z.rows, z.vpad, z.lanes), f32)]
        + [shape((inner, z.lanes), f32)],
        (own, right, left, paired),
        [
            pltpu.VMEM((2 * z.rows, z.pick_rows, z.lanes), f32),
            pltpu.VMEM((2 * z.rows, z.pick_rows, z.lanes), f32),
            pltpu.VMEM((inner, z.vpad, z.lanes), f32),
            pltpu.VMEM((z.message - z.value_at, z.lanes), f32),
        ],
    )
    bands = lax.axis_size("lat")
    one = lax.ppermute(first, ("lat", "lon"), swaps(bands, count, 0))
    two = lax.ppermute(second, ("lat", "lon"), swaps(bands, count, 1))
    packed, outer_picks, offset_rows = call(
        "forward",
        functools.partial(forward_kernel, z),
        [
            shape((z.packed, z.lanes), f32),
            shape((outer, z.lanes), f32),
            shape((up_to(3 * z.dest, 8), LANES), f32),
        ],
        (whole, one, two, narrow, product, partial),
        [
            pltpu.VMEM((z.blocks, z.pick_rows, z.lanes), f32),
            pltpu.VMEM((z.blocks, z.pick_rows, z.lanes), f32),
            pltpu.VMEM((4, z.wrows, z.lanes), f32),
            pltpu.VMEM((outer, z.vpad, z.lanes), f32),
        ],
    )
    members = lax.axis_size("ens")
    others = []
    for k in range(1, members):
        if members & (members - 1):
            route = [(i, (i + k) % members) for i in range(members)]
        else:
            route = [(i, i ^ k) for i in range(members)]
        others.append(lax.ppermute(packed, "ens", route))
    base, scale, shared_picks = call(
        "observe",
        functools.partial(observation_kernel, z, members),
        [shape((z.packed, z.lanes), f32)] * 2 + [shape((z.slots, max(z.shared, 8), z.lanes), f32)],
        (whole, one, two, packed, inner_picks, outer_picks),
    )
    (result,) = call(
        "backward",
        functools.partial(backward_kernel, z, members),
        [shape(hidden.shape, f32)],
        (packed, *others, base, scale, inner_picks, outer_picks, shared_picks, offset_rows, turned),
        [
            pltpu.VMEM((z.packed, z.lanes), f32),
            pltpu.VMEM((z.packed, z.lanes), f32),
            pltpu.VMEM((z.blocks, 8, z.lanes), f32),
            pltpu.VMEM((z.blocks, 8, z.lanes), f32),
            pltpu.VMEM((z.slots, max(z.shared, 8), z.lanes), f32),
            pltpu.VMEM((z.bases * max(z.full, 8), z.lanes), f32),
            pltpu.VMEM((z.bases * max(z.full, 8), z.lanes), f32),
            pltpu.VMEM((z.bases * max(z.shared, 8), z.lanes), f32),
            pltpu.VMEM((z.depth, z.lanes), bf16),
            pltpu.VMEM((z.depth, z.lanes), bf16),
            pltpu.VMEM(hidden.shape[1:], f32),
            pltpu.SemaphoreType.DMA((3,)),
        ],
        out_specs=(HBM,),
    )
    return result


def solution(mesh):
    return jax.shard_map(
        on_device,
        mesh=mesh,
        in_specs=(
            P("ens", None, "lat", "lon"),
            P(),
            P(None, "lat"),
            P(None, "lat", "lon"),
            P(None, "lat", "lon"),
            P("lat"),
        ),
        out_specs=P("ens", None, "lat", "lon"),
        check_vma=False,
    )
```

```python
import functools

import jax
import jax.numpy as jnp
from jax import lax
from jax.experimental import pallas as pl
from jax.experimental.pallas import tpu as pltpu
from jax.sharding import PartitionSpec as P

SPAN = 4
MARGIN = SPAN + 1
LANES = 128
SUB = 16
VMEM_LIMIT = 16 * 2**20

smooth_square = 0.01

f32 = jnp.float32
bf16 = jnp.bfloat16
VMEM = pl.BlockSpec(memory_space=pltpu.VMEM)
HBM = pl.BlockSpec(memory_space=pltpu.HBM)


def up_to(n, step):
    return -(-n // step) * step


class Sizes:
    def __init__(self, hidden, filt):
        _, self.channels, self.rows, self.cols = hidden.shape
        self.bases, self.variables, _ = filt.shape
        self.slots = 9
        self.lanes = up_to(self.cols + 2 * MARGIN, LANES)
        self.rim = (self.cols - MARGIN) // LANES * LANES
        self.paired = up_to(self.channels * self.rows, SUB)
        self.latent = up_to(self.channels, SUB)
        self.latents = self.paired
        self.pick_rows = up_to(self.slots + 5, SUB)
        self.obs_rows = up_to(self.variables, SUB)
        self.half = self.pick_rows + 2 * self.obs_rows
        self.table = 2 * self.half
        self.table_at = self.paired
        self.own_rows = self.table_at + self.rows * self.table
        self.dest = self.rows + 2
        self.vpad = up_to(self.variables, SUB)
        self.wrows = self.bases * self.vpad
        self.blocks = 2 * self.dest
        self.full = self.variables // 8 * 8
        self.rest = self.variables - self.full
        self.packed = up_to(self.blocks * self.variables, 8)
        self.value_rows = up_to(4 * self.variables, 8)
        self.head_at = self.latent
        self.value_at = self.head_at + SUB
        self.message = self.value_at + up_to(2 * self.value_rows, SUB)
        self.shared = up_to(2 * self.rows * self.rest, 8)
        self.shared_at = self.rows * self.bases * self.full
        self.depth = up_to(self.shared_at + self.bases * self.shared, SUB)
        inner = range(1, self.rows + 1)
        self.inner = [(i, a) for i in inner for a in (-1, 0, 1) if i + a in inner]
        self.outer = [(0, 1), (self.dest - 1, -1), (1, -1), (self.rows, 1)]

    def block(self, n, count):
        ranges = []
        if self.full:
            ranges.append((slice(n * self.full, (n + 1) * self.full), slice(0, self.full)))
        if self.rest:
            at = count * self.full + n * self.rest
            ranges.append((slice(at, at + self.rest), slice(self.full, self.variables)))
        return ranges

    def own_table(self, i, parity, start):
        return self.table_at + (i - 1) * self.table + parity * self.half + start


def lane_step(z, x, step, to_right):
    amount = step if to_right else lax.bitwise_and(LANES - step, LANES - 1)
    parts = [pltpu.roll(x[:, at : at + LANES], amount, axis=1) for at in range(0, z.lanes, LANES)]
    lane = lax.broadcasted_iota(jnp.int32, parts[0].shape, 1)
    enters = lane < step if to_right else lane >= LANES - step
    near = -1 if to_right else 1
    return jnp.concatenate(
        [
            jnp.where(enters, parts[(n + near) % len(parts)], part)
            for n, part in enumerate(parts)
        ],
        axis=1,
    )


def scalar_of(row):
    return jnp.max(row).astype(jnp.int32)


def steps(direction, offset, parity):
    other = lax.rem(parity + offset, 2)
    shift = lax.shift_right_arithmetic(direction * offset + other - parity, 1)
    return other, direction * shift


def selection(shape, hit):
    row = lax.broadcasted_iota(jnp.int32, shape, 0)
    col = lax.broadcasted_iota(jnp.int32, shape, 1)
    return hit(row, col).astype(f32).astype(bf16)


def matmul(a, b):
    return jnp.dot(a, b, preferred_element_type=f32)


def is_odd_band():
    return lax.rem(lax.axis_index("lat"), 2) == 1


def prepare_kernel(z, *refs):
    arguments, (own, edge, work), local, arrived = refs[:5], refs[5:8], refs[8:13], refs[13]
    copies = []
    for n in range(5):
        copies.append(pltpu.make_async_copy(arguments[n], local[n], arrived.at[n]))
        copies[n].start()
    hidden, pick, obs, offsets, cosine = local
    wide = 2 * LANES
    split = selection(
        (wide, wide), lambda r, c: r == jnp.where(c < LANES, 2 * c, 2 * (c - LANES) + 1)
    )
    work[...] = jnp.zeros_like(work)
    for copy in copies[1:]:
        copy.wait()
    grid = 2 * z.cols
    for i in range(z.rows):
        work[0 : z.slots, 0:grid] = pick[:, i, :].astype(f32)
        o = obs[:, i, :]
        high = o.astype(bf16).astype(f32)
        work[z.pick_rows : z.pick_rows + z.variables, 0:grid] = high
        low_at = z.pick_rows + z.obs_rows
        work[low_at : low_at + z.variables, 0:grid] = o - high
        for t in range(3):
            work[z.slots + t : z.slots + t + 1, :] = jnp.broadcast_to(
                offsets[i : i + 1, t : t + 1].astype(f32), (1, work.shape[1])
            )
        c = cosine[0:1, i : i + 1]
        c_high = c.astype(bf16).astype(f32)
        work[z.slots + 3 : z.slots + 4, :] = jnp.broadcast_to(c_high, (1, work.shape[1]))
        work[z.slots + 4 : z.slots + 5, :] = jnp.broadcast_to(c - c_high, (1, work.shape[1]))
        at = z.table_at + i * z.table
        for n in range(z.lanes // LANES):
            parts = matmul(work[:, n * wide : (n + 1) * wide].astype(bf16), split).astype(bf16)
            for parity in range(2):
                own[at + parity * z.half : at + (parity + 1) * z.half, n * LANES : (n + 1) * LANES] = (
                    parts[:, parity * LANES : (parity + 1) * LANES]
                )
    copies[0].wait()
    pairs = z.channels * z.rows
    own[0 : z.paired] = jnp.pad(
        hidden[0].reshape(pairs, z.cols), ((0, z.paired - pairs), (0, z.lanes - z.cols))
    )
    width = z.lanes - z.rim
    lane = lax.broadcasted_iota(jnp.int32, (z.own_rows, width), 1)
    first = pltpu.roll(own[:, 0:width].astype(f32), z.cols - z.rim, axis=1)
    last = pltpu.roll(own[:, z.rim :].astype(f32), z.lanes - z.cols, axis=1)
    ahead = (lane >= z.cols - z.rim) & (lane < z.cols - z.rim + MARGIN)
    behind = lane >= width - MARGIN
    edge[...] = jnp.where(ahead, first, jnp.where(behind, last, 0.0)).astype(bf16)


def weights_kernel(z, filt, narrow, paired, turned, work, spread_out):
    work[...] = jnp.zeros_like(work)
    for k in range(z.bases):
        work[k * z.vpad : k * z.vpad + z.variables, 0 : z.channels] = filt[k].astype(f32)
    flat = work[...].astype(bf16)
    narrow[...] = flat
    total = None
    for i in range(z.rows):
        spread = selection((z.latent, z.paired), lambda r, c: c == r * z.rows + i)
        paired[i * z.wrows : (i + 1) * z.wrows] = matmul(flat, spread).astype(bf16)
        spread_out[...] = jnp.zeros_like(spread_out)
        for k in range(z.bases):
            w = work[k * z.vpad : k * z.vpad + z.variables]
            if z.full:
                at = (i * z.bases + k) * z.full
                spread_out[at : at + z.full] = w[0 : z.full]
            for parity in range(2):
                if z.rest:
                    at = z.shared_at + k * z.shared + (2 * i + parity) * z.rest
                    spread_out[at : at + z.rest] = w[z.full :]
        turned_spread = selection((z.paired, z.latent), lambda r, c: r == c * z.rows + i)
        part = lax.dot_general(
            turned_spread,
            spread_out[...].astype(bf16),
            (((1,), (1,)), ((), ())),
            preferred_element_type=f32,
        )
        total = part if total is None else total + part
    turned[...] = total.astype(bf16)


def halfway(z, latents):
    h = latents.astype(f32)
    return (0.5 * (h + pltpu.roll(h, z.lanes - 1, axis=1))).astype(bf16)


def choose(z, product, at, work, picks, chosen, first=0):
    for lane in range(0, z.lanes, LANES):
        span = slice(lane, lane + LANES)
        pick = [jnp.broadcast_to(picks[n - first : n - first + 1, span], (8, LANES)) for n in work]
        best = {}
        for k in range(z.bases):
            mask = [p == float(k) for p in pick] if k else None
            for v in range(0, z.variables, 8):
                value = product[at, k * z.vpad + v : k * z.vpad + v + 8, span]
                for m in range(len(work)):
                    best[m, v] = jnp.where(mask[m], value, best[m, v]) if k else value
        for m, n in enumerate(work):
            for v in range(0, z.variables, 8):
                chosen[n, v : v + 8, span] = best[m, v]


def row_picks(z, pairs, offset, pick_rows, picks):
    for at, (i, a) in enumerate(pairs):
        for b in (-1, 0, 1):
            for parity in range(2):
                n = (3 * at + b + 1) * 2 + parity
                if b == 0:
                    picks[n : n + 1, :] = pick_rows(i, a, b, parity)
                    continue
                other, step = steps(b, offset(i, a), parity)
                picks[n : n + 1, :] = lane_step(z, pick_rows(i, a, b, other), step, b > 0)


def collect(z, pairs, offset, chosen, i, parity):
    total = None
    for at, (row, a) in enumerate(pairs):
        if row != i:
            continue
        for b in (-1, 0, 1):
            if b == 0:
                value = chosen[(3 * at + 1) * 2 + parity]
            else:
                other, step = steps(-b, offset(i, a), parity)
                value = lane_step(z, chosen[(3 * at + b + 1) * 2 + other], step, b < 0)
            total = value if total is None else total + value
    return total


def own_kernel(z, own, right, left, weight, whole, one, two, product, partial, picks, table, chosen, values):
    whole[:, 0 : z.rim] = own[:, 0 : z.rim]
    width = z.lanes - z.rim
    lane = lax.broadcasted_iota(jnp.int32, (z.own_rows, width), 1)
    outer = jnp.where(lane >= width - MARGIN, left[...].astype(f32), right[...].astype(f32))
    inner = own[:, z.rim :].astype(f32)
    whole[:, z.rim :] = jnp.where(lane < z.cols - z.rim, inner, outer).astype(bf16)

    for i in range(1, z.rows + 1):
        for parity in range(2):
            at = z.own_table(i, parity, 0)
            table[2 * i - 2 + parity] = whole[at : at + z.pick_rows].astype(f32)
    offsets = {
        (i, a): scalar_of(table[2 * i - 2, z.slots + a + 1 : z.slots + a + 2, 0:LANES])
        for i, a in z.inner
    }

    def offset(i, a):
        return offsets[i, a]

    def pick_rows(i, a, b, parity):
        slot = 3 * (a + 1) + b + 1
        return table[2 * i - 2 + parity, slot : slot + 1, :]

    latents = whole[0 : z.paired]
    for parity, x in enumerate((latents, halfway(z, latents))):
        both = matmul(weight[...], x)
        for i in range(z.rows):
            product[2 * i + parity] = both[i * z.wrows : (i + 1) * z.wrows]
    row_picks(z, z.inner, offset, pick_rows, picks)
    for s in range(1, z.rows + 1):
        for parity in range(2):
            work = [
                (3 * at + b) * 2 + parity
                for at, (i, a) in enumerate(z.inner)
                for b in range(3)
                if i + a == s
            ]
            choose(z, product, 2 * s - 2 + parity, work, picks, chosen)
    for i in range(1, z.rows + 1):
        for parity in range(2):
            partial[2 * i - 2 + parity] = collect(z, z.inner, offset, chosen, i, parity)

    odd = is_odd_band()

    def head(i, a):
        slot = 3 * (a + 1)
        return (
            [table[2 * i - 2 + parity, slot : slot + 3, :] for parity in range(2)]
            + [table[2 * i - 2, z.slots + a + 1 : z.slots + a + 2, :]]
            + [table[2 * i - 2, z.slots + 3 : z.slots + 5, :]]
        )

    def blocks(i):
        result = []
        for parity in range(2):
            at = z.own_table(i, parity, z.pick_rows)
            high = whole[at : at + z.obs_rows].astype(f32)
            low = whole[at + z.obs_rows : at + 2 * z.obs_rows].astype(f32)
            result.append(high + low)
        return result + [partial[2 * i - 2 + parity] for parity in range(2)]

    down, up = (z.rows, 1), (1, -1)
    heads = head(*down), head(*up)
    bodies = blocks(z.rows), blocks(1)
    for m, message in ((0, one), (1, two)):
        goes_up = odd if m == 0 else jnp.logical_not(odd)
        row = jnp.where(goes_up, 0, z.rows - 1)
        boundary = selection((z.latent, z.paired), lambda r, c: c == r * z.rows + row)
        message[0 : z.latent] = matmul(boundary, latents).astype(bf16)
        values[...] = jnp.zeros_like(values)
        at = 0
        for d, u in zip(*heads):
            values[at : at + d.shape[0]] = jnp.where(goes_up, u, d)
            at += d.shape[0]
        message[z.head_at : z.value_at] = values[0:SUB].astype(bf16)
        values[0:SUB] = jnp.zeros_like(values[0:SUB])
        for n, (d, u) in enumerate(zip(*bodies)):
            value = jnp.where(goes_up, u, d)
            high = value.astype(bf16).astype(f32)
            for packed_rows, rows in z.block(n, 4):
                values[packed_rows] = high[rows]
                low_rows = slice(packed_rows.start + z.value_rows, packed_rows.stop + z.value_rows)
                values[low_rows] = (value - high)[rows]
        message[z.value_at :] = values[...].astype(bf16)


def near_values(z, one, two, start, count):
    odd = is_odd_band()
    band = lax.axis_index("lat")
    a, b = one[start : start + count].astype(f32), two[start : start + count].astype(f32)
    above, below = jnp.where(odd, a, b), jnp.where(odd, b, a)
    return (
        jnp.where(band > 0, above, 0.0),
        jnp.where(band < lax.axis_size("lat") - 1, below, 0.0),
    )


def near_block(z, values, n):
    result = []
    for packed_rows, rows in z.block(n, 4):
        low_rows = slice(packed_rows.start + z.value_rows, packed_rows.stop + z.value_rows)
        result.append((rows, values[packed_rows] + values[low_rows]))
    return result


def rim_picks_kernel(z, whole, picks, offset_rows, table):
    offset_rows[...] = jnp.zeros_like(offset_rows)
    for i in range(1, z.rows + 1):
        for parity in range(2):
            at = z.own_table(i, parity, 0)
            table[2 * i - 2 + parity] = whole[at : at + z.pick_rows].astype(f32)
        for t in range(3):
            offset_rows[3 * i + t : 3 * i + t + 1] = table[2 * i - 2, z.slots + t : z.slots + t + 1, 0:LANES]
    pairs = z.outer[2:]
    offsets = {
        (i, a): scalar_of(offset_rows[3 * i + a + 1 : 3 * i + a + 2]) for i, a in pairs
    }

    def pick_rows(i, a, b, parity):
        slot = 3 * (a + 1) + b + 1
        return table[2 * i - 2 + parity, slot : slot + 1, :]

    row_picks(z, pairs, lambda i, a: offsets[i, a], pick_rows, picks)


def forward_kernel(z, whole, one, two, weight, own_product, partial, rim_picks, own_offsets, packed, picks, offset_rows, table, product, chosen):
    heads = near_values(z, one, two, z.head_at, SUB)
    offset_rows[...] = own_offsets[...]
    for n, (i, a) in enumerate(z.outer[:2]):
        offset_rows[3 * i + a + 1 : 3 * i + a + 2] = heads[n][6:7, 0:LANES]
        for parity in range(2):
            table[2 * n + parity, 0:3] = heads[n][3 * parity : 3 * parity + 3]
    offsets = {
        (i, a): scalar_of(offset_rows[3 * i + a + 1 : 3 * i + a + 2]) for i, a in z.outer
    }

    def offset(i, a):
        return offsets[i, a]

    def pick_rows(i, a, b, parity):
        return table[(2 if i else 0) + parity, b + 1 : b + 2, :]

    latents = near_values(z, one, two, 0, z.latent)
    for n in range(2):
        x = latents[n].astype(bf16)
        product[2 * n] = matmul(weight[...], x)
        product[2 * n + 1] = matmul(weight[...], halfway(z, x))
    row_picks(z, z.outer[:2], offset, pick_rows, picks)
    for at, (i, a) in enumerate(z.outer):
        s = i + a
        for parity in range(2):
            work = [(3 * at + b) * 2 + parity for b in range(3)]
            if s in (0, z.dest - 1):
                choose(z, product, (2 if s else 0) + parity, work, rim_picks, chosen, 12)
            else:
                choose(z, own_product, 2 * s - 2 + parity, work, picks, chosen)
    if z.packed != z.blocks * z.variables:
        packed[...] = jnp.zeros_like(packed)
    bodies = near_values(z, one, two, z.value_at, 2 * z.value_rows)
    for i in range(z.dest):
        for parity in range(2):
            total = collect(z, z.outer, offset, chosen, i, parity)
            if 0 < i < z.dest - 1:
                before = partial[2 * i - 2 + parity]
                total = before if total is None else before + total
                for packed_rows, rows in z.block(2 * i + parity, z.blocks):
                    packed[packed_rows] = total[rows]
            else:
                before = near_block(z, bodies[1 if i else 0], 2 + parity)
                for (packed_rows, rows), (_, value) in zip(z.block(2 * i + parity, z.blocks), before):
                    packed[packed_rows] = total[rows] + value


def smoothed_derivative(difference):
    return difference * lax.rsqrt(difference * difference + smooth_square)


def observation_kernel(z, members, whole, one, two, packed, inner_picks, outer_picks, base, scale, shared):
    shared[...] = jnp.zeros_like(shared)
    for picks, i, a, n in gradient_sources(z, inner_picks, outer_picks):
        for b in (-1, 0, 1):
            for parity in range(2):
                row = picks[n + 2 * (b + 1) + parity : n + 2 * (b + 1) + parity + 1, :]
                if z.rest:
                    at = (2 * (i + a - 1) + parity) * z.rest
                    shared[3 * (a + 1) + b + 1, at : at + z.rest] = jnp.broadcast_to(row, (z.rest, z.lanes))
    if z.packed != z.blocks * z.variables:
        base[...] = jnp.zeros_like(base)
        scale[...] = jnp.zeros_like(scale)
    heads = near_values(z, one, two, z.head_at, SUB)
    bodies = near_values(z, one, two, z.value_at, 2 * z.value_rows)
    for i in range(z.dest):
        if 0 < i < z.dest - 1:
            at = z.own_table(i, 0, 0)
            first = whole[at : at + z.pick_rows].astype(f32)
            cosine = first[z.slots + 3 : z.slots + 4] + first[z.slots + 4 : z.slots + 5]
        else:
            first = heads[1 if i else 0]
            cosine = first[7:8] + first[8:9]
        for parity in range(2):
            if 0 < i < z.dest - 1:
                at = z.own_table(i, parity, z.pick_rows)
                high = whole[at : at + z.obs_rows].astype(f32)
                low = whole[at + z.obs_rows : at + 2 * z.obs_rows].astype(f32)
                seen = [(high + low)[rows] for _, rows in z.block(0, 1)]
            else:
                seen = [value for _, value in near_block(z, bodies[1 if i else 0], parity)]
            for (rows, _), value in zip(z.block(2 * i + parity, z.blocks), seen):
                weight = jnp.broadcast_to(cosine, value.shape)
                base[rows] = weight * smoothed_derivative(packed[rows] - value)
                scale[rows] = weight * (1.0 / max(members - 1, 1))


def gradient_sources(z, inner_picks, outer_picks):
    result = []
    for picks, pairs in ((inner_picks, z.inner), (outer_picks, z.outer[:2])):
        for at, (i, a) in enumerate(pairs):
            result.append((picks, i, a, 6 * at))
    return result


def backward_kernel(z, members, *refs):
    mine, others = refs[0], refs[1:members]
    base, scale, inner_picks, outer_picks, shared_picks, offset_rows, weight = refs[members : members + 7]
    out, flat, rest, shared, even, odd, extra, hi, lo, stage, sent = refs[members + 7 :]
    sources = gradient_sources(z, inner_picks, outer_picks)
    offset = {
        (i, a): scalar_of(offset_rows[3 * i + a + 1 : 3 * i + a + 2]) for _, i, a, _ in sources
    }
    value = mine[...]
    pairs = jnp.zeros_like(value)
    for other in others:
        pairs = pairs + smoothed_derivative(value - other[...])
    gradient = base[...] - scale[...] * pairs
    flat[...] = gradient
    if z.rest:
        rest[...] = jnp.zeros_like(rest)
        for block in range(z.blocks):
            at = z.blocks * z.full + block * z.rest
            rest[block, 0 : z.rest] = flat[at : at + z.rest]
        shared[...] = jnp.zeros_like(shared)

    moved, pick = {}, {}
    for picks, i, a, n in sources:
        j = i + a
        for b in (-1, 0, 1):
            for parity in range(2):
                key = j, parity, a, b
                at = n + 2 * (b + 1) + parity
                pick[key] = picks[at : at + 1, :]
                block = 2 * i + parity
                if b == 0:
                    if z.full:
                        moved[key] = flat[block * z.full : (block + 1) * z.full]
                    if z.rest:
                        tail = rest[block]
                else:
                    other, step = steps(b, offset[i, a], parity)
                    block = 2 * i + other
                    if z.full:
                        rows = pl.ds(pl.multiple_of(block * z.full, 8), z.full)
                        moved[key] = lane_step(z, flat[rows], step, b > 0)
                    if z.rest:
                        tail = lane_step(z, rest[block], step, b > 0)
                if z.rest:
                    at = (2 * (j - 1) + parity) * z.rest
                    shared[3 * (a + 1) + b + 1, at : at + z.rest] = tail[0 : z.rest]

    def gather(terms, k):
        total = None
        for value, p in terms:
            term = jnp.where(p == float(k), value, 0.0)
            total = term if total is None else total + term
        return total

    def keep(rows, total):
        top = total.astype(bf16)
        hi[rows] = top
        lo[rows] = (total - top.astype(f32)).astype(bf16)

    hi[z.shared_at :] = jnp.zeros_like(hi[z.shared_at :])
    lo[z.shared_at :] = jnp.zeros_like(lo[z.shared_at :])
    if z.full:
        for j in range(1, z.rows + 1):
            for at in range(0, z.lanes, LANES):
                span = slice(at, at + LANES)
                for parity, part in ((0, even), (1, odd)):
                    keys = [key for key in pick if key[:2] == (j, parity)]
                    wide = [jnp.broadcast_to(pick[key][:, span], (8, LANES)) for key in keys]
                    for v in range(0, z.full, 8):
                        terms = [(moved[key][v : v + 8, span], p) for key, p in zip(keys, wide)]
                        for k in range(z.bases):
                            part[k * z.full + v : k * z.full + v + 8, span] = gather(terms, k)
            half = odd[...]
            total = even[...] + 0.5 * (half + pltpu.roll(half, 1, axis=1))
            at = (j - 1) * z.bases * z.full
            keep(slice(at, at + z.bases * z.full), total)
    if z.rest:
        for at in range(0, z.lanes, LANES):
            span = slice(at, at + LANES)
            for v in range(0, z.shared, 8):
                terms = [
                    (shared[slot, v : v + 8, span], shared_picks[slot, v : v + 8, span])
                    for slot in range(z.slots)
                ]
                for k in range(z.bases):
                    extra[k * z.shared + v : k * z.shared + v + 8, span] = gather(terms, k)
        total = extra[...]
        row = lax.rem(lax.broadcasted_iota(jnp.int32, total.shape, 0), z.shared)
        is_odd = lax.rem(lax.div(row, z.rest), 2) == 1
        total = jnp.where(is_odd, 0.5 * (total + pltpu.roll(total, 1, axis=1)), total)
        keep(slice(z.shared_at, z.shared_at + z.bases * z.shared), total)

    pieces = 3
    length = up_to(-(-z.channels // pieces), SUB // 2)
    copies = []
    for first in range(0, z.channels, length):
        last = min(first + length, z.channels)
        w = weight[first * z.rows : up_to(last * z.rows, SUB)]
        field = matmul(w, hi[...]) + matmul(w, lo[...])
        count = last - first
        stage[first:last] = field[0 : count * z.rows, 0 : z.cols].reshape(count, z.rows, z.cols)
        copy = pltpu.make_async_copy(
            stage.at[first:last], out.at[0, first:last], sent.at[len(copies)]
        )
        copy.start()
        copies.append(copy)
    for copy in copies:
        copy.wait()


def swaps(bands, sectors, start):
    pairs = []
    for i in range(bands):
        other = i + 1 if (i - start) % 2 == 0 else i - 1
        for j in range(sectors):
            if 0 <= other < bands:
                pairs.append((i * sectors + j, other * sectors + j))
            else:
                pairs.append((i * sectors + j, i * sectors + (j + 1) % sectors))
    return pairs


def call(name, kernel, outs, inputs, scratch=(), in_specs=None, out_specs=None, flops=10_000_000):
    size = sum(x.size * x.dtype.itemsize for x in tuple(inputs) + tuple(outs))
    return pl.pallas_call(
        kernel,
        name=name,
        out_shape=tuple(outs),
        in_specs=in_specs or [VMEM] * len(inputs),
        out_specs=out_specs or tuple([VMEM] * len(outs)),
        scratch_shapes=list(scratch),
        compiler_params=pltpu.CompilerParams(vmem_limit_bytes=VMEM_LIMIT),
        cost_estimate=pl.CostEstimate(flops=flops, bytes_accessed=size, transcendentals=0),
    )(*inputs)


def on_device(hidden, filt, offsets, pick, observation, cosine):
    z = Sizes(hidden, filt)
    shape = jax.ShapeDtypeStruct
    arguments = (hidden, pick, observation, offsets.T, cosine[None])
    arguments = tuple(pltpu.with_memory_space_constraint(x, pltpu.HBM) for x in arguments)
    own, edge = call(
        "prepare",
        functools.partial(prepare_kernel, z),
        [shape((z.own_rows, z.lanes), bf16), shape((z.own_rows, z.lanes - z.rim), bf16)],
        arguments,
        [pltpu.VMEM((z.half, 2 * z.lanes), f32)]
        + [pltpu.VMEM(x.shape, x.dtype) for x in arguments]
        + [pltpu.SemaphoreType.DMA((5,))],
        in_specs=[HBM] * 5,
    )
    narrow, paired, turned = call(
        "weights",
        functools.partial(weights_kernel, z),
        [
            shape((z.wrows, z.latent), bf16),
            shape((z.rows * z.wrows, z.paired), bf16),
            shape((z.paired, z.depth), bf16),
        ],
        (filt,),
        [pltpu.VMEM((z.wrows, z.latent), f32), pltpu.VMEM((z.depth, z.latent), f32)],
    )
    count = lax.axis_size("lon")
    right = lax.ppermute(edge, "lon", [((i + 1) % count, i) for i in range(count)])
    left = right
    if count != 2:
        left = lax.ppermute(edge, "lon", [(i, (i + 1) % count) for i in range(count)])
    inner, outer = 6 * len(z.inner), 6 * len(z.outer)
    whole, first, second, product, partial, inner_picks = call(
        "own",
        functools.partial(own_kernel, z),
        [shape((z.own_rows, z.lanes), bf16)]
        + [shape((z.message, z.lanes), bf16)] * 2
        + [shape((2 * z.rows, z.wrows, z.lanes), f32)]
        + [shape((2 * z.rows, z.vpad, z.lanes), f32)]
        + [shape((inner, z.lanes), f32)],
        (own, right, left, paired),
        [
            pltpu.VMEM((2 * z.rows, z.pick_rows, z.lanes), f32),
            pltpu.VMEM((inner, z.vpad, z.lanes), f32),
            pltpu.VMEM((z.message - z.value_at, z.lanes), f32),
        ],
    )
    bands = lax.axis_size("lat")
    one = lax.ppermute(first, ("lat", "lon"), swaps(bands, count, 0))
    two = lax.ppermute(second, ("lat", "lon"), swaps(bands, count, 1))
    offset_shape = shape((up_to(3 * z.dest, 8), LANES), f32)
    rim_picks, own_offsets = call(
        "rim_picks",
        functools.partial(rim_picks_kernel, z),
        [shape((up_to(outer // 2, 8), z.lanes), f32), offset_shape],
        (whole,),
        [pltpu.VMEM((2 * z.rows, z.pick_rows, z.lanes), f32)],
    )
    packed, outer_picks, offset_rows = call(
        "forward",
        functools.partial(forward_kernel, z),
        [
            shape((z.packed, z.lanes), f32),
            shape((up_to(outer // 2, 8), z.lanes), f32),
            offset_shape,
        ],
        (whole, one, two, narrow, product, partial, rim_picks, own_offsets),
        [
            pltpu.VMEM((4, 8, z.lanes), f32),
            pltpu.VMEM((4, z.wrows, z.lanes), f32),
            pltpu.VMEM((outer, z.vpad, z.lanes), f32),
        ],
    )
    members = lax.axis_size("ens")
    others = []
    for k in range(1, members):
        if members & (members - 1):
            route = [(i, (i + k) % members) for i in range(members)]
        else:
            route = [(i, i ^ k) for i in range(members)]
        others.append(lax.ppermute(packed, "ens", route))
    base, scale, shared_picks = call(
        "observe",
        functools.partial(observation_kernel, z, members),
        [shape((z.packed, z.lanes), f32)] * 2 + [shape((z.slots, max(z.shared, 8), z.lanes), f32)],
        (whole, one, two, packed, inner_picks, outer_picks),
    )
    (result,) = call(
        "backward",
        functools.partial(backward_kernel, z, members),
        [shape(hidden.shape, f32)],
        (packed, *others, base, scale, inner_picks, outer_picks, shared_picks, offset_rows, turned),
        [
            pltpu.VMEM((z.packed, z.lanes), f32),
            pltpu.VMEM((z.blocks, 8, z.lanes), f32),
            pltpu.VMEM((z.slots, max(z.shared, 8), z.lanes), f32),
            pltpu.VMEM((z.bases * max(z.full, 8), z.lanes), f32),
            pltpu.VMEM((z.bases * max(z.full, 8), z.lanes), f32),
            pltpu.VMEM((z.bases * max(z.shared, 8), z.lanes), f32),
            pltpu.VMEM((z.depth, z.lanes), bf16),
            pltpu.VMEM((z.depth, z.lanes), bf16),
            pltpu.VMEM(hidden.shape[1:], f32),
            pltpu.SemaphoreType.DMA((3,)),
        ],
        out_specs=(HBM,),
    )
    return result


def solution(mesh):
    return jax.shard_map(
        on_device,
        mesh=mesh,
        in_specs=(
            P("ens", None, "lat", "lon"),
            P(),
            P(None, "lat"),
            P(None, "lat", "lon"),
            P(None, "lat", "lon"),
            P("lat"),
        ),
        out_specs=P("ens", None, "lat", "lon"),
        check_vma=False,
    )
```
